256 devices in a mesh: section: 4 (over x), blk: 64 (over y, z, core).
Axes of the slice: x: 4, y: 4, z: 8, core: 2. Of those that a mesh axis runs over, the one named last changes fastest.
Arguments:
- inputs: bfloat16 [4096, 8192], P(None, 'blk'), may hold values from -6 to 6
- cotangent: bfloat16 [4096, 8192], P(None, 'blk'), may hold values from -6 to 6
- r_weight: bfloat16 [4, 64, 128, 128], P('section', 'blk'), may hold values from -0.5 to 0.5
- g_weight: bfloat16 [4, 64, 128, 128], P('section', 'blk'), may hold values from -0.5 to 0.5
- l_weight: bfloat16 [4, 128, 64, 64], P('section', 'blk'), may hold values from -0.75 to 0.75
Outputs:
- input_grad: bfloat16 [4, 4096, 8192], P('section', None, 'blk')
- r_grad: float32 [4, 64, 128, 128], P('section', 'blk')
- g_grad: float32 [4, 64, 128, 128], P('section', 'blk')
- l_grad: float32 [4, 128, 64, 64], P('section', 'blk')
The draws below stay inside these ranges and needn't reach their ends.
All inputs are finite; a program needn't handle non-finite values.
Results may differ from the reference program's by a relative error of at most 0.014.
Values may be sent and summed in bfloat16 or wider, within the bound.
No kernel may reach another device: no remote copies, remote signals or barrier semaphores. Data moves between devices by JAX's collectives and lax.ppermute only.
A program may use at most 192 MiB of HBM per device.

```python
import jax
import jax.numpy as jnp

BLOCKS = 64
BSIZE = 128
TOKENS = 4096
SECTIONS = 4
D = 8192
N_SECTION = 4


def level_of(rng, extent, shards, least, high):
    def one(dim, shards_of):
        draws = jax.random.uniform(jax.random.fold_in(jax.random.fold_in(rng, 6), dim), (shards_of,), jnp.float32, least / len(shards), high / len(shards))
        return jnp.repeat(jnp.exp(draws), extent[dim] // shards_of).reshape((-1,) + (1,) * (len(extent) - dim - 1))

    level = one(*shards[0])
    for cut in shards[1:]:
        level = level * one(*cut)
    return level


def scatter_about(key, shape, deviation, most, split=(), held_as=jnp.bfloat16):
    array = deviation * jax.random.normal(key, shape, jnp.float32)
    if split:
        array = array * level_of(key, shape, split, -0.22, 0.18)
    return jnp.clip(array, -most, most).astype(held_as)


def setup_inputs(seed: int = 0) -> dict:
    arg_keys = jax.random.split(jax.random.key(seed), 6)
    inputs = scatter_about(arg_keys[0], (TOKENS, D), 1.0, 6.0, ((1, 64),))
    cotangent = scatter_about(arg_keys[1], (TOKENS, D), 1.0, 6.0, ((1, 64),))
    r_weight = scatter_about(arg_keys[2], (SECTIONS, BLOCKS, BSIZE, BSIZE), BSIZE ** -0.5, 0.5, ((0, 4), (1, 64)))
    g_weight = scatter_about(arg_keys[3], (SECTIONS, BLOCKS, BSIZE, BSIZE), BSIZE ** -0.5, 0.5, ((0, 4), (1, 64)))
    l_weight = scatter_about(arg_keys[4], (SECTIONS, BSIZE, BLOCKS, BLOCKS), BLOCKS ** -0.5, 0.75, ((0, 4), (1, 64)))
    return {"inputs": inputs, "cotangent": cotangent, "r_weight": r_weight, "g_weight": g_weight, "l_weight": l_weight}


def reference(inputs, cotangent, r_weight, g_weight, l_weight):
    f32 = jnp.float32
    bf16 = jnp.bfloat16
    count = inputs.shape[0]
    current = inputs
    stored = []
    for layer in range(N_SECTION):
        blocks = current.reshape(count, BLOCKS, BSIZE)
        first = jnp.einsum("nbj,bjk->nbk", blocks.astype(f32), r_weight[layer].astype(f32)).astype(bf16)
        mixed = jnp.einsum("nbk,kbc->nck", first.astype(f32), l_weight[layer].astype(f32)).astype(bf16)
        gate = jnp.einsum("nbj,bjk->nbk", blocks.astype(f32), g_weight[layer].astype(f32))
        current = (blocks.astype(f32) + mixed.astype(f32) * jax.nn.sigmoid(gate)).astype(bf16).reshape(count, -1)
        stored.append((blocks, first, mixed))
    upper = cotangent
    grads_in = []
    r_list = []
    g_list = []
    l_list = []
    for layer in range(N_SECTION - 1, -1, -1):
        blocks, first, mixed = stored[layer]
        gate = jnp.einsum("nbj,bjk->nbk", blocks.astype(f32), g_weight[layer].astype(f32))
        sig = jax.nn.sigmoid(gate)
        upper_f = upper.reshape(count, BLOCKS, BSIZE).astype(f32)
        grad_mixed = (upper_f * sig).astype(bf16)
        grad_gate = (upper_f * mixed.astype(f32) * sig * (1.0 - sig)).astype(bf16)
        grad_first = jnp.einsum("nck,kbc->nbk", grad_mixed.astype(f32), l_weight[layer].astype(f32)).astype(bf16)
        lower = upper_f + jnp.einsum("nbk,bjk->nbj", grad_first.astype(f32), r_weight[layer].astype(f32))
        lower = lower + jnp.einsum("nbk,bjk->nbj", grad_gate.astype(f32), g_weight[layer].astype(f32))
        upper = lower.astype(bf16).reshape(count, -1)
        grads_in.append(upper)
        r_list.append(jnp.einsum("nbj,nbk->bjk", blocks.astype(f32), grad_first.astype(f32)))
        g_list.append(jnp.einsum("nbj,nbk->bjk", blocks.astype(f32), grad_gate.astype(f32)))
        l_list.append(jnp.einsum("nbk,nck->kbc", first.astype(f32), grad_mixed.astype(f32)))
    return (jnp.stack(grads_in[::-1]), jnp.stack(r_list[::-1]), jnp.stack(g_list[::-1]), jnp.stack(l_list[::-1]))
```

```python
import functools

import jax
import jax.numpy as jnp
from jax import lax
from jax.experimental import pallas as pl
from jax.experimental.pallas import tpu as pltpu
from jax.sharding import Mesh, PartitionSpec as P

BF = jnp.bfloat16
F32 = jnp.float32
CHUNKS = 2


def nn(a, b):
    return lax.dot_general(a, b, (((1,), (0,)), ((), ())), preferred_element_type=F32)


def nt(a, b):
    return lax.dot_general(a, b, (((1,), (1,)), ((), ())), preferred_element_type=F32)


def feature_order(rows, cols, transposed=False):
    r = lax.broadcasted_iota(jnp.int32, (rows, cols), 1 if transposed else 0)
    c = lax.broadcasted_iota(jnp.int32, (rows, cols), 0 if transposed else 1)
    natural = ((r >> 2) & 1) * 128 + (r >> 3) * 4 + (r & 3)
    return jnp.where(natural == c, 1.0, 0.0).astype(BF)


def position_order(rows, cols, transposed=False):
    r = lax.broadcasted_iota(jnp.int32, (rows, cols), 1 if transposed else 0)
    c = lax.broadcasted_iota(jnp.int32, (rows, cols), 0 if transposed else 1)
    natural = (r & 3) * 64 + (r >> 3) * 2 + ((r >> 2) & 1)
    return jnp.where(natural == c, 1.0, 0.0).astype(BF)


def rows_of(ref):
    d, i, n = ref.shape
    return ref[...].astype(F32).reshape(d * i, n)


def put_rows(ref, value):
    ref[...] = value.reshape(ref.shape).astype(ref.dtype)


def prepare_kernel(w_ref, r_ref, rt_ref, g_ref, gt_ref, l_ref, lt_ref):
    p = feature_order(256, 256)
    q = position_order(256, 256)
    for start, plain, flipped in ((0, r_ref, rt_ref), (128, g_ref, gt_ref)):
        blocks = [w_ref[c, start : start + 128, :] for c in range(2)]
        parts = [p[:, 128 * c : 128 * c + 128] for c in range(2)]
        left = jnp.concatenate([nn(parts[c], blocks[c]) for c in range(2)], axis=1).astype(BF)
        plain[...] = nt(left, p).astype(BF)
        left = jnp.concatenate([nt(parts[c], blocks[c]) for c in range(2)], axis=1).astype(BF)
        flipped[...] = nt(left, p).astype(BF)
    lane = lax.broadcasted_iota(jnp.int32, (64, 128), 1)
    pairs = []
    for c in range(2):
        packed = w_ref[c, 256:320, :].astype(F32)
        pairs.append(
            jnp.concatenate(
                [jnp.where(lane < 64, packed, 0.0), jnp.where(lane < 64, 0.0, packed)], axis=0
            ).astype(BF)
        )
    parts = [q[:, 128 * c : 128 * c + 128] for c in range(2)]
    left = jnp.concatenate([nn(parts[c], pairs[c]) for c in range(2)], axis=1).astype(BF)
    l_ref[...] = nt(left, q).astype(BF)
    left = jnp.concatenate([nt(parts[c], pairs[c]) for c in range(2)], axis=1).astype(BF)
    lt_ref[...] = nt(left, q).astype(BF)


def turn_kernel(x_ref, o_ref):
    p = feature_order(256, 256)
    o_ref[...] = (nt(p[:, :128], x_ref[0]) + nt(p[:, 128:], x_ref[1])).astype(BF)


def first_kernel(x_ref, rt_ref, z_ref):
    put_rows(z_ref, nn(rt_ref[...], x_ref[...]))


def mix_kernel(z_ref, w_ref, u_ref):
    put_rows(u_ref, nn(w_ref[...], rows_of(z_ref).astype(BF)))


def gated_kernel(x_ref, u_ref, gt_ref, rt_ref, x_out, z_ref):
    x = x_ref[...]
    sig = jax.nn.sigmoid(nn(gt_ref[...], x))
    new = (x.astype(F32) + rows_of(u_ref) * sig).astype(BF)
    x_out[...] = new
    put_rows(z_ref, nn(rt_ref[...], new))


def gate_back(upper, x, u, gt, gu_ref, gg_ref):
    sig = jax.nn.sigmoid(nn(gt, x))
    put_rows(gu_ref, upper * sig)
    gg_ref[...] = (upper * u * sig * (1.0 - sig)).astype(BF)


def back_start_kernel(y_ref, x_ref, u_ref, gt_ref, gu_ref, gg_ref):
    gate_back(y_ref[...].astype(F32), x_ref[...], rows_of(u_ref), gt_ref[...], gu_ref, gg_ref)


def lower_of(y_ref, gz_ref, gg_ref, r_ref, g_ref):
    gz = rows_of(gz_ref).astype(BF)
    lower = y_ref[...].astype(F32) + nn(r_ref[...], gz)
    return (lower + nn(g_ref[...], gg_ref[...])).astype(BF)


def back_kernel(y_ref, gz_ref, gg_ref, r_ref, g_ref, x_ref, u_ref, gt_ref, y_out, gu_ref, gg_out):
    lower = lower_of(y_ref, gz_ref, gg_ref, r_ref, g_ref)
    y_out[...] = lower
    gate_back(lower.astype(F32), x_ref[...], rows_of(u_ref), gt_ref[...], gu_ref, gg_out)


def back_end_kernel(y_ref, gz_ref, gg_ref, r_ref, g_ref, y_out):
    y_out[...] = lower_of(y_ref, gz_ref, gg_ref, r_ref, g_ref)


def grads_kernel(*refs):
    ins, (w_out, y_out) = refs[:-2], refs[-2:]
    pt = feature_order(256, 256, True)
    qt = position_order(256, 256, True)
    r_sum = g_sum = l_sum = None
    n = ins[0].shape[-1]
    for c in range(CHUNKS):
        x, gz, gg, z, gu, y = ins[6 * c : 6 * c + 6]
        x_n = nn(pt, x[...]).astype(BF)
        gz_n = nn(pt, rows_of(gz).astype(BF)).astype(BF)
        gg_n = nn(pt, gg[...]).astype(BF)
        z_n = nn(qt, rows_of(z).astype(BF)).astype(BF)
        gu_n = nn(qt, rows_of(gu).astype(BF)).astype(BF)
        y_n = nn(pt, y[...])
        r_c = [nt(x_n[128 * i : 128 * i + 128], gz_n[128 * i : 128 * i + 128]) for i in range(2)]
        g_c = [nt(x_n[128 * i : 128 * i + 128], gg_n[128 * i : 128 * i + 128]) for i in range(2)]
        l_c = [nt(z_n[128 * i : 128 * i + 128], gu_n[128 * i : 128 * i + 128]) for i in range(2)]
        if r_sum is None:
            r_sum, g_sum, l_sum = r_c, g_c, l_c
        else:
            r_sum = [a + b for a, b in zip(r_sum, r_c)]
            g_sum = [a + b for a, b in zip(g_sum, g_c)]
            l_sum = [a + b for a, b in zip(l_sum, l_c)]
        for i in range(2):
            y_out[i, n * c : n * c + n, :] = y_n[128 * i : 128 * i + 128].T.astype(BF)
    lane = lax.broadcasted_iota(jnp.int32, (64, 128), 1)
    for i in range(2):
        w_out[i, 0:128, :] = r_sum[i].astype(w_out.dtype)
        w_out[i, 128:256, :] = g_sum[i].astype(w_out.dtype)
        w_out[i, 256:320, :] = jnp.where(lane < 64, l_sum[i][:64], l_sum[i][64:]).astype(w_out.dtype)


def run(kernel, outs, *args, dots=1):
    n = args[0].shape[-1]
    nbytes = sum(a.size * a.dtype.itemsize for a in args)
    return pl.pallas_call(
        kernel,
        out_shape=outs,
        compiler_params=pltpu.CompilerParams(vmem_limit_bytes=16 << 20),
        cost_estimate=pl.CostEstimate(
            flops=dots * 2 * 256 * 256 * n, bytes_accessed=2 * nbytes, transcendentals=0
        ),
    )(*args)


def sds(*shape, dtype=BF):
    return jax.ShapeDtypeStruct(shape, dtype)


def shards(inputs, cotangent, r_weight, g_weight, l_weight):
    layers = r_weight.shape[0] * lax.axis_size("x")
    tokens = inputs.shape[0] // (lax.axis_size("x") * 2)
    n = tokens // CHUNKS
    sect = lax.axis_index("x")
    core = lax.axis_index("c")

    l_flat = jnp.concatenate([l_weight[0, 0], l_weight[0, 1]], axis=1)
    packed = jnp.concatenate([r_weight[0, 0], g_weight[0, 0], l_flat], axis=0)
    every = lax.all_gather(packed, ("x", "c"), axis=0, tiled=False)
    every = every.reshape(layers, 2, 320, 128)
    mats = [run(prepare_kernel, [sds(256, 256)] * 6, every[s]) for s in range(layers)]

    def own_part(whole):
        mine = lax.dynamic_slice_in_dim(whole, (sect * 2 + core) * tokens, tokens, 0)
        other = lax.dynamic_slice_in_dim(whole, (sect * 2 + 1 - core) * tokens, tokens, 0)
        other = lax.ppermute(other, "c", [(0, 1), (1, 0)])
        low = jnp.where(core == 0, mine, other)
        high = jnp.where(core == 0, other, mine)
        pair = jnp.stack([low, high])
        return [run(turn_kernel, sds(256, n), pair[:, i * n : i * n + n]) for i in range(CHUNKS)]

    def swap(block):
        return lax.all_to_all(block, ("y", "z"), 0, 0, tiled=True)

    flat = sds(256, n)
    sent = sds(32, 8, n)
    ids = range(CHUNKS)
    x = [own_part(inputs)]
    y = own_part(cotangent)
    z_all, u_all = [], []
    z = [run(first_kernel, sent, x[0][i], mats[0][1]) for i in ids]
    for s in range(layers):
        z = [swap(z[i]) for i in ids]
        z_all.append(z)
        u = [swap(run(mix_kernel, sent, z[i], mats[s][5])) for i in ids]
        u_all.append(u)
        if s + 1 < layers:
            both = [
                run(gated_kernel, [flat, sent], x[s][i], u[i], mats[s][3], mats[s + 1][1], dots=2)
                for i in ids
            ]
            x.append([b[0] for b in both])
            z = [b[1] for b in both]
    last = layers - 1
    both = [
        run(back_start_kernel, [sent, flat], y[i], x[last][i], u_all[last][i], mats[last][3])
        for i in ids
    ]
    gu = [b[0] for b in both]
    gg = [b[1] for b in both]
    w_parts, y_parts = [], []
    for s in range(last, -1, -1):
        gu = [swap(gu[i]) for i in ids]
        gz = [swap(run(mix_kernel, sent, gu[i], mats[s][4])) for i in ids]
        held = (x[s], gz, gg, z_all[s], gu)
        if s > 0:
            trio = [
                run(
                    back_kernel,
                    [flat, sent, flat],
                    y[i],
                    gz[i],
                    gg[i],
                    mats[s][0],
                    mats[s][2],
                    x[s - 1][i],
                    u_all[s - 1][i],
                    mats[s - 1][3],
                    dots=3,
                )
                for i in ids
            ]
            y = [t[0] for t in trio]
            gu = [t[1] for t in trio]
            gg = [t[2] for t in trio]
        else:
            y = [
                run(back_end_kernel, flat, y[i], gz[i], gg[i], mats[s][0], mats[s][2], dots=2)
                for i in ids
            ]
        args = []
        for i in ids:
            args += [a[i] for a in held] + [y[i]]
        w_part, y_part = run(
            grads_kernel, [sds(2, 320, 128), sds(2, tokens, 128)], *args, dots=12
        )
        w_parts.insert(0, w_part)
        y_parts.insert(0, y_part)

    w_sent = jnp.stack(w_parts).reshape(layers * 2, 320, 128)
    y_sent = jnp.stack(y_parts).reshape(layers * 2, tokens, 128)
    y_back = lax.all_to_all(y_sent, ("x", "c"), 0, 0, tiled=True)
    w_back = lax.all_to_all(w_sent, ("x", "c"), 0, 0, tiled=True)
    total = jnp.sum(w_back.astype(F32), axis=0)
    r_grad, g_grad, l_flat = total[:128], total[128:256], total[256:]
    l_grad = jnp.stack([l_flat[:, :64], l_flat[:, 64:]])
    return (
        y_back.reshape(1, layers * 2 * tokens, 128),
        r_grad[None, None],
        g_grad[None, None],
        l_grad[None],
    )


def solution(mesh):
    grid = Mesh(mesh.devices.reshape(4, 4, 8, 2), ("x", "y", "z", "c"))
    blk = ("y", "z", "c")
    return jax.shard_map(
        shards,
        mesh=grid,
        in_specs=(
            P(None, blk),
            P(None, blk),
            P("x", blk, None, None),
            P("x", blk, None, None),
            P("x", blk, None, None),
        ),
        out_specs=(
            P("x", None, blk),
            P("x", blk, None, None),
            P("x", blk, None, None),
            P("x", blk, None, None),
        ),
        check_vma=False,
    )
```

```python
import functools

import jax
import jax.numpy as jnp
from jax import lax
from jax.experimental import pallas as pl
from jax.experimental.pallas import tpu as pltpu
from jax.sharding import Mesh, PartitionSpec as P

BF = jnp.bfloat16
F32 = jnp.float32
CHUNKS = 1


def nn(a, b):
    return lax.dot_general(a, b, (((1,), (0,)), ((), ())), preferred_element_type=F32)


def nt(a, b):
    return lax.dot_general(a, b, (((1,), (1,)), ((), ())), preferred_element_type=F32)


def feature_order(rows, cols, transposed=False):
    r = lax.broadcasted_iota(jnp.int32, (rows, cols), 1 if transposed else 0)
    c = lax.broadcasted_iota(jnp.int32, (rows, cols), 0 if transposed else 1)
    natural = ((r >> 2) & 1) * 128 + (r >> 3) * 4 + (r & 3)
    return jnp.where(natural == c, 1.0, 0.0).astype(BF)


def position_order(rows, cols, transposed=False):
    r = lax.broadcasted_iota(jnp.int32, (rows, cols), 1 if transposed else 0)
    c = lax.broadcasted_iota(jnp.int32, (rows, cols), 0 if transposed else 1)
    natural = (r & 3) * 64 + (r >> 3) * 2 + ((r >> 2) & 1)
    return jnp.where(natural == c, 1.0, 0.0).astype(BF)


def rows_of(ref):
    d, i, n = ref.shape
    return ref[...].astype(F32).reshape(d * i, n)


def put_rows(ref, value):
    ref[...] = value.reshape(ref.shape).astype(ref.dtype)


def prepare_kernel(w_ref, r_ref, rt_ref, g_ref, gt_ref, l_ref, lt_ref):
    p = feature_order(256, 256)
    q = position_order(256, 256)
    for start, plain, flipped in ((0, r_ref, rt_ref), (128, g_ref, gt_ref)):
        blocks = [w_ref[c, start : start + 128, :] for c in range(2)]
        parts = [p[:, 128 * c : 128 * c + 128] for c in range(2)]
        left = jnp.concatenate([nn(parts[c], blocks[c]) for c in range(2)], axis=1).astype(BF)
        plain[...] = nt(left, p).astype(BF)
        left = jnp.concatenate([nt(parts[c], blocks[c]) for c in range(2)], axis=1).astype(BF)
        flipped[...] = nt(left, p).astype(BF)
    lane = lax.broadcasted_iota(jnp.int32, (64, 128), 1)
    pairs = []
    for c in range(2):
        packed = w_ref[c, 256:320, :].astype(F32)
        pairs.append(
            jnp.concatenate(
                [jnp.where(lane < 64, packed, 0.0), jnp.where(lane < 64, 0.0, packed)], axis=0
            ).astype(BF)
        )
    parts = [q[:, 128 * c : 128 * c + 128] for c in range(2)]
    left = jnp.concatenate([nn(parts[c], pairs[c]) for c in range(2)], axis=1).astype(BF)
    l_ref[...] = nt(left, q).astype(BF)
    left = jnp.concatenate([nt(parts[c], pairs[c]) for c in range(2)], axis=1).astype(BF)
    lt_ref[...] = nt(left, q).astype(BF)


def turn_kernel(x_ref, o_ref):
    p = feature_order(256, 256)
    o_ref[...] = (nt(p[:, :128], x_ref[0]) + nt(p[:, 128:], x_ref[1])).astype(BF)


def first_kernel(x_ref, rt_ref, z_ref):
    put_rows(z_ref, nn(rt_ref[...], x_ref[...]))


def mix_kernel(z_ref, w_ref, u_ref):
    put_rows(u_ref, nn(w_ref[...], rows_of(z_ref).astype(BF)))


def gated_kernel(x_ref, u_ref, gt_ref, rt_ref, x_out, z_ref):
    x = x_ref[...]
    sig = jax.nn.sigmoid(nn(gt_ref[...], x))
    new = (x.astype(F32) + rows_of(u_ref) * sig).astype(BF)
    x_out[...] = new
    put_rows(z_ref, nn(rt_ref[...], new))


def gate_back(upper, x, u, gt, gu_ref, gg_ref):
    sig = jax.nn.sigmoid(nn(gt, x))
    put_rows(gu_ref, upper * sig)
    gg_ref[...] = (upper * u * sig * (1.0 - sig)).astype(BF)


def back_start_kernel(y_ref, x_ref, u_ref, gt_ref, gu_ref, gg_ref):
    gate_back(y_ref[...].astype(F32), x_ref[...], rows_of(u_ref), gt_ref[...], gu_ref, gg_ref)


def lower_of(y_ref, gz_ref, gg_ref, r_ref, g_ref):
    gz = rows_of(gz_ref).astype(BF)
    lower = y_ref[...].astype(F32) + nn(r_ref[...], gz)
    return (lower + nn(g_ref[...], gg_ref[...])).astype(BF)


def back_kernel(y_ref, gz_ref, gg_ref, r_ref, g_ref, x_ref, u_ref, gt_ref, y_out, gu_ref, gg_out):
    lower = lower_of(y_ref, gz_ref, gg_ref, r_ref, g_ref)
    y_out[...] = lower
    gate_back(lower.astype(F32), x_ref[...], rows_of(u_ref), gt_ref[...], gu_ref, gg_out)


def back_end_kernel(y_ref, gz_ref, gg_ref, r_ref, g_ref, y_out):
    y_out[...] = lower_of(y_ref, gz_ref, gg_ref, r_ref, g_ref)


def grads_kernel(*refs):
    ins, (w_out, y_out) = refs[:-2], refs[-2:]
    pt = feature_order(256, 256, True)
    qt = position_order(256, 256, True)
    r_sum = g_sum = l_sum = None
    n = ins[0].shape[-1]
    for c in range(CHUNKS):
        x, gz, gg, z, gu, y = ins[6 * c : 6 * c + 6]
        x_n = nn(pt, x[...]).astype(BF)
        gz_n = nn(pt, rows_of(gz).astype(BF)).astype(BF)
        gg_n = nn(pt, gg[...]).astype(BF)
        z_n = nn(qt, rows_of(z).astype(BF)).astype(BF)
        gu_n = nn(qt, rows_of(gu).astype(BF)).astype(BF)
        y_n = nn(pt, y[...])
        r_c = [nt(x_n[128 * i : 128 * i + 128], gz_n[128 * i : 128 * i + 128]) for i in range(2)]
        g_c = [nt(x_n[128 * i : 128 * i + 128], gg_n[128 * i : 128 * i + 128]) for i in range(2)]
        l_c = [nt(z_n[128 * i : 128 * i + 128], gu_n[128 * i : 128 * i + 128]) for i in range(2)]
        if r_sum is None:
            r_sum, g_sum, l_sum = r_c, g_c, l_c
        else:
            r_sum = [a + b for a, b in zip(r_sum, r_c)]
            g_sum = [a + b for a, b in zip(g_sum, g_c)]
            l_sum = [a + b for a, b in zip(l_sum, l_c)]
        for i in range(2):
            y_out[i, n * c : n * c + n, :] = y_n[128 * i : 128 * i + 128].T.astype(BF)
    lane = lax.broadcasted_iota(jnp.int32, (64, 128), 1)
    for i in range(2):
        w_out[i, 0:128, :] = r_sum[i].astype(w_out.dtype)
        w_out[i, 128:256, :] = g_sum[i].astype(w_out.dtype)
        w_out[i, 256:320, :] = jnp.where(lane < 64, l_sum[i][:64], l_sum[i][64:]).astype(w_out.dtype)


def run(kernel, outs, *args, dots=1):
    n = args[0].shape[-1]
    nbytes = sum(a.size * a.dtype.itemsize for a in args)
    return pl.pallas_call(
        kernel,
        out_shape=outs,
        compiler_params=pltpu.CompilerParams(vmem_limit_bytes=16 << 20),
        cost_estimate=pl.CostEstimate(
            flops=dots * 2 * 256 * 256 * n, bytes_accessed=2 * nbytes, transcendentals=0
        ),
    )(*args)


def sds(*shape, dtype=BF):
    return jax.ShapeDtypeStruct(shape, dtype)


def shards(inputs, cotangent, r_weight, g_weight, l_weight):
    layers = r_weight.shape[0] * lax.axis_size("x")
    tokens = inputs.shape[0] // (lax.axis_size("x") * 2)
    n = tokens // CHUNKS
    sect = lax.axis_index("x")
    core = lax.axis_index("c")

    l_flat = jnp.concatenate([l_weight[0, 0], l_weight[0, 1]], axis=1)
    packed = jnp.concatenate([r_weight[0, 0], g_weight[0, 0], l_flat], axis=0)
    every = lax.all_gather(packed, ("x", "c"), axis=0, tiled=False)
    every = every.reshape(layers, 2, 320, 128)
    mats = [run(prepare_kernel, [sds(256, 256)] * 6, every[s]) for s in range(layers)]

    def own_part(whole):
        mine = lax.dynamic_slice_in_dim(whole, (sect * 2 + core) * tokens, tokens, 0)
        other = lax.dynamic_slice_in_dim(whole, (sect * 2 + 1 - core) * tokens, tokens, 0)
        other = lax.ppermute(other, "c", [(0, 1), (1, 0)])
        low = jnp.where(core == 0, mine, other)
        high = jnp.where(core == 0, other, mine)
        pair = jnp.stack([low, high])
        return [run(turn_kernel, sds(256, n), pair[:, i * n : i * n + n]) for i in range(CHUNKS)]

    def swap(block):
        return lax.all_to_all(block, ("y", "z"), 0, 0, tiled=True)

    flat = sds(256, n)
    sent = sds(32, 8, n)
    ids = range(CHUNKS)
    x = [own_part(inputs)]
    y = own_part(cotangent)
    z_all, u_all = [], []
    z = [run(first_kernel, sent, x[0][i], mats[0][1]) for i in ids]
    for s in range(layers):
        z = [swap(z[i]) for i in ids]
        z_all.append(z)
        u = [swap(run(mix_kernel, sent, z[i], mats[s][5])) for i in ids]
        u_all.append(u)
        if s + 1 < layers:
            both = [
                run(gated_kernel, [flat, sent], x[s][i], u[i], mats[s][3], mats[s + 1][1], dots=2)
                for i in ids
            ]
            x.append([b[0] for b in both])
            z = [b[1] for b in both]
    last = layers - 1
    both = [
        run(back_start_kernel, [sent, flat], y[i], x[last][i], u_all[last][i], mats[last][3])
        for i in ids
    ]
    gu = [b[0] for b in both]
    gg = [b[1] for b in both]
    w_parts, y_parts = [], []
    for s in range(last, -1, -1):
        gu = [swap(gu[i]) for i in ids]
        gz = [swap(run(mix_kernel, sent, gu[i], mats[s][4])) for i in ids]
        held = (x[s], gz, gg, z_all[s], gu)
        if s > 0:
            trio = [
                run(
                    back_kernel,
                    [flat, sent, flat],
                    y[i],
                    gz[i],
                    gg[i],
                    mats[s][0],
                    mats[s][2],
                    x[s - 1][i],
                    u_all[s - 1][i],
                    mats[s - 1][3],
                    dots=3,
                )
                for i in ids
            ]
            y = [t[0] for t in trio]
            gu = [t[1] for t in trio]
            gg = [t[2] for t in trio]
        else:
            y = [
                run(back_end_kernel, flat, y[i], gz[i], gg[i], mats[s][0], mats[s][2], dots=2)
                for i in ids
            ]
        args = []
        for i in ids:
            args += [a[i] for a in held] + [y[i]]
        w_part, y_part = run(
            grads_kernel, [sds(2, 320, 128), sds(2, tokens, 128)], *args, dots=12
        )
        w_parts.insert(0, w_part)
        y_parts.insert(0, y_part)

    w_sent = jnp.stack(w_parts).reshape(layers * 2, 320, 128)
    y_sent = jnp.stack(y_parts).reshape(layers * 2, tokens, 128)
    y_back = lax.all_to_all(y_sent, ("x", "c"), 0, 0, tiled=True)
    w_back = lax.all_to_all(w_sent, ("x", "c"), 0, 0, tiled=True)
    total = jnp.sum(w_back.astype(F32), axis=0)
    r_grad, g_grad, l_flat = total[:128], total[128:256], total[256:]
    l_grad = jnp.stack([l_flat[:, :64], l_flat[:, 64:]])
    return (
        y_back.reshape(1, layers * 2 * tokens, 128),
        r_grad[None, None],
        g_grad[None, None],
        l_grad[None],
    )


def solution(mesh):
    grid = Mesh(mesh.devices.reshape(4, 4, 8, 2), ("x", "y", "z", "c"))
    blk = ("y", "z", "c")
    return jax.shard_map(
        shards,
        mesh=grid,
        in_specs=(
            P(None, blk),
            P(None, blk),
            P("x", blk, None, None),
            P("x", blk, None, None),
            P("x", blk, None, None),
        ),
        out_specs=(
            P("x", None, blk),
            P("x", blk, None, None),
            P("x", blk, None, None),
            P("x", blk, None, None),
        ),
        check_vma=False,
    )
```

```python
import jax
import jax.numpy as jnp
from jax import lax
from jax.experimental import pallas as pl
from jax.experimental.pallas import tpu as pltpu
from jax.sharding import Mesh, PartitionSpec as P

BF = jnp.bfloat16
F32 = jnp.float32


def nn(a, b):
    return lax.dot_general(a, b, (((1,), (0,)), ((), ())), preferred_element_type=F32)


def nt(a, b):
    return lax.dot_general(a, b, (((1,), (1,)), ((), ())), preferred_element_type=F32)


def feature_order(rows, cols, transposed=False, offset=0):
    r = lax.broadcasted_iota(jnp.int32, (rows, cols), 1 if transposed else 0)
    c = lax.broadcasted_iota(jnp.int32, (rows, cols), 0 if transposed else 1)
    natural = ((r >> 2) & 1) * 128 + (r >> 3) * 4 + (r & 3)
    return jnp.where(natural == c + offset, 1.0, 0.0).astype(BF)


def position_order(rows, cols, transposed=False):
    r = lax.broadcasted_iota(jnp.int32, (rows, cols), 1 if transposed else 0)
    c = lax.broadcasted_iota(jnp.int32, (rows, cols), 0 if transposed else 1)
    natural = (r & 3) * 64 + (r >> 3) * 2 + ((r >> 2) & 1)
    return jnp.where(natural == c, 1.0, 0.0).astype(BF)


def rows_of(ref):
    d, i, n = ref.shape
    return ref[...].astype(F32).reshape(d * i, n)


def put_rows(ref, value):
    ref[...] = value.reshape(ref.shape).astype(ref.dtype)


def block_of(own_ref, other_ref, c, core, k, start, stop):
    mine = own_ref[k, start:stop, :].astype(F32)
    other = other_ref[k, start:stop, :].astype(F32)
    return jnp.where(core == c, mine, other)


def prepare_kernel(at_ref, *refs):
    shifted, other_ref = refs[:4], refs[4]
    outs, own_ref = refs[5:-1], refs[-1]
    sect, core = at_ref[0], at_ref[1]
    for k in range(4):
        own_ref[k] = shifted[k][...]
    p = feature_order(256, 256)
    q = position_order(256, 256)
    lane = lax.broadcasted_iota(jnp.int32, (64, 128), 1)
    for layer in range(4):
        k = lax.rem(sect - layer + 4, 4)
        r_out, rt_out, g_out, gt_out, l_out, lt_out = outs[6 * layer : 6 * layer + 6]
        for start, plain, flipped in ((0, r_out, rt_out), (128, g_out, gt_out)):
            blocks = [
                block_of(own_ref, other_ref, c, core, k, start, start + 128).astype(BF)
                for c in range(2)
            ]
            parts = [p[:, 128 * c : 128 * c + 128] for c in range(2)]
            left = jnp.concatenate([nn(parts[c], blocks[c]) for c in range(2)], axis=1).astype(BF)
            plain[...] = nt(left, p).astype(BF)
            left = jnp.concatenate([nt(parts[c], blocks[c]) for c in range(2)], axis=1).astype(BF)
            flipped[...] = nt(left, p).astype(BF)
        pairs = []
        for c in range(2):
            packed = block_of(own_ref, other_ref, c, core, k, 256, 320)
            low = jnp.where(lane < 64, packed, 0.0)
            high = jnp.where(lane < 64, 0.0, packed)
            pairs.append(jnp.concatenate([low, high], axis=0).astype(BF))
        parts = [q[:, 128 * c : 128 * c + 128] for c in range(2)]
        left = jnp.concatenate([nn(parts[c], pairs[c]) for c in range(2)], axis=1).astype(BF)
        l_out[...] = nt(left, q).astype(BF)
        left = jnp.concatenate([nt(parts[c], pairs[c]) for c in range(2)], axis=1).astype(BF)
        lt_out[...] = nt(left, q).astype(BF)


def turned(core, mine_ref, other_ref):
    p = feature_order(256, 128, offset=core * 128)
    o = feature_order(256, 128, offset=128 - core * 128)
    return (nt(p, mine_ref[...]) + nt(o, other_ref[...])).astype(BF)


def turn_kernel(at_ref, mine_ref, other_ref, o_ref):
    o_ref[...] = turned(at_ref[1], mine_ref, other_ref)


def first_kernel(at_ref, mine_ref, other_ref, rt_ref, x_ref, z_ref):
    x = turned(at_ref[1], mine_ref, other_ref)
    x_ref[...] = x
    put_rows(z_ref, nn(rt_ref[...], x))


def mix_kernel(z_ref, w_ref, u_ref):
    put_rows(u_ref, nn(w_ref[...], rows_of(z_ref).astype(BF)))


def gated_kernel(x_ref, u_ref, gt_ref, rt_ref, x_out, z_ref):
    x = x_ref[...]
    sig = jax.nn.sigmoid(nn(gt_ref[...], x))
    new = (x.astype(F32) + rows_of(u_ref) * sig).astype(BF)
    x_out[...] = new
    put_rows(z_ref, nn(rt_ref[...], new))


def gate_back(upper, x, u, gt, gu_ref, gg_ref):
    sig = jax.nn.sigmoid(nn(gt, x))
    put_rows(gu_ref, upper * sig)
    gg_ref[...] = (upper * u * sig * (1.0 - sig)).astype(BF)


def back_start_kernel(y_ref, x_ref, u_ref, gt_ref, gu_ref, gg_ref):
    gate_back(y_ref[...].astype(F32), x_ref[...], rows_of(u_ref), gt_ref[...], gu_ref, gg_ref)


def lower_of(y_ref, gz_ref, gg_ref, r_ref, g_ref):
    gz = rows_of(gz_ref).astype(BF)
    lower = y_ref[...].astype(F32) + nn(r_ref[...], gz)
    return (lower + nn(g_ref[...], gg_ref[...])).astype(BF)


def back_kernel(y_ref, gz_ref, gg_ref, r_ref, g_ref, x_ref, u_ref, gt_ref, y_out, gu_ref, gg_out):
    lower = lower_of(y_ref, gz_ref, gg_ref, r_ref, g_ref)
    y_out[...] = lower
    gate_back(lower.astype(F32), x_ref[...], rows_of(u_ref), gt_ref[...], gu_ref, gg_out)


def parts_of(x, gz, gg, z, gu, y):
    pt = feature_order(256, 256, True)
    qt = position_order(256, 256, True)
    x_n = nn(pt, x).astype(BF)
    gz_n = nn(pt, gz).astype(BF)
    gg_n = nn(pt, gg).astype(BF)
    z_n = nn(qt, z).astype(BF)
    gu_n = nn(qt, gu).astype(BF)
    y_n = nn(pt, y)
    lane = lax.broadcasted_iota(jnp.int32, (64, 128), 1)
    parts = []
    for i in range(2):
        at = slice(128 * i, 128 * i + 128)
        l_part = nt(z_n[at], gu_n[at])
        parts.append(
            (
                y_n[at].T,
                nt(x_n[at], gz_n[at]),
                nt(x_n[at], gg_n[at]),
                jnp.where(lane < 64, l_part[:64], l_part[64:]),
            )
        )
    return parts


def put_parts(core, parts, mine_out, other_out):
    start = 0
    for low, high in zip(*parts):
        stop = start + low.shape[0]
        mine_out[start:stop, :] = jnp.where(core == 0, low, high).astype(BF)
        other_out[start:stop, :] = jnp.where(core == 0, high, low).astype(BF)
        start = stop


def parts_kernel(at_ref, x_ref, gz_ref, gg_ref, z_ref, gu_ref, y_ref, mine_out, other_out):
    parts = parts_of(
        x_ref[...],
        rows_of(gz_ref).astype(BF),
        gg_ref[...],
        rows_of(z_ref).astype(BF),
        rows_of(gu_ref).astype(BF),
        y_ref[...],
    )
    put_parts(at_ref[1], parts, mine_out, other_out)


def last_kernel(
    at_ref, x_ref, gz_ref, gg_ref, z_ref, gu_ref, y_ref, r_ref, g_ref, mine_out, other_out
):
    lower = lower_of(y_ref, gz_ref, gg_ref, r_ref, g_ref)
    parts = parts_of(
        x_ref[...],
        rows_of(gz_ref).astype(BF),
        gg_ref[...],
        rows_of(z_ref).astype(BF),
        rows_of(gu_ref).astype(BF),
        lower,
    )
    put_parts(at_ref[1], parts, mine_out, other_out)


def join(core, mine_ref, other_ref, out_ref):
    n = (out_ref.shape[0] - 320) // 2
    out_ref[pl.ds(pl.multiple_of(core * n, n), n), :] = mine_ref[:n, :]
    out_ref[pl.ds(pl.multiple_of((1 - core) * n, n), n), :] = other_ref[:n, :]
    total = mine_ref[n:, :].astype(F32) + other_ref[n:, :].astype(F32)
    out_ref[2 * n :, :] = total.astype(BF)


def join_kernel(at_ref, mine_ref, other_ref, out_ref):
    join(at_ref[1], mine_ref, other_ref, out_ref)


def route_kernel(at_ref, *refs):
    sect, core = at_ref[0], at_ref[1]
    mine, other, outs = refs[:3], refs[3:6], refs[6:]
    for k in range(4):
        target = lax.rem(sect + k, 4)

        @pl.when(target == 0)
        def _():
            outs[k][...] = jnp.zeros_like(outs[k])

        for layer in range(1, 4):

            @pl.when(target == layer)
            def _():
                join(core, mine[layer - 1], other[layer - 1], outs[k])


def settle_kernel(at_ref, *refs):
    early, late = refs[:4], refs[4:8]
    y_out, r_out, g_out, l_out = refs[8:]
    sect = at_ref[0]
    n = y_out.shape[0] // 4

    def settle(parts):
        total = None
        for k in range(4):
            source = pl.multiple_of(lax.rem(sect - k + 4, 4) * n, n)
            y_out[pl.ds(source, n), :] = parts[k][:n, :]
            part = parts[k][n:, :].astype(F32)
            total = part if total is None else total + part
        r_out[...] = total[:128]
        g_out[...] = total[128:256]
        l_out[0] = total[256:, :64]
        l_out[1] = total[256:, 64:]

    @pl.when(sect == 0)
    def _():
        settle(late)

    @pl.when(sect != 0)
    def _():
        settle(early)


def run(kernel, outs, *args, dots=1, at=None, scratch=(), blocks=None):
    nbytes = sum(a.size * a.dtype.itemsize for a in args)
    params = pltpu.CompilerParams(vmem_limit_bytes=16 << 20)
    cost = pl.CostEstimate(
        flops=dots * 2 * 256 * 256 * 512, bytes_accessed=2 * nbytes, transcendentals=0
    )
    if at is None:
        return pl.pallas_call(
            kernel, out_shape=outs, compiler_params=params, cost_estimate=cost
        )(*args)
    specs = [
        spec or pl.BlockSpec(a.shape, lambda i, at, nd=a.ndim: (0,) * nd)
        for a, spec in zip(args, blocks or [None] * len(args))
    ]
    many = isinstance(outs, list)
    out_specs = [
        pl.BlockSpec(o.shape, lambda i, at, nd=len(o.shape): (0,) * nd)
        for o in (outs if many else [outs])
    ]
    return pl.pallas_call(
        kernel,
        out_shape=outs,
        grid_spec=pltpu.PrefetchScalarGridSpec(
            num_scalar_prefetch=1,
            grid=(1,),
            in_specs=specs,
            out_specs=out_specs if many else out_specs[0],
            scratch_shapes=list(scratch),
        ),
        compiler_params=params,
        cost_estimate=cost,
    )(at, *args)


def sds(*shape, dtype=BF):
    return jax.ShapeDtypeStruct(shape, dtype)


def shards(inputs, cotangent, r_weight, g_weight, l_weight):
    sections = lax.axis_size("x")
    tokens = inputs.shape[0] // (sections * 2)
    sect = lax.axis_index("x")
    core = lax.axis_index("c")
    at = jnp.stack([sect, core, sect * 2 + core]).astype(jnp.int32)

    def to_other(value):
        return lax.ppermute(value, "c", [(0, 1), (1, 0)])

    def shift(value, k, targets=range(4)):
        route = [(i, (i + k) % sections) for i in range(sections)]
        return lax.ppermute(value, "x", [(i, j) for i, j in route if j in targets])

    l_flat = jnp.concatenate([l_weight[0, 0], l_weight[0, 1]], axis=1)
    packed = jnp.concatenate([r_weight[0, 0], g_weight[0, 0], l_flat], axis=0)
    own = [packed] + [shift(packed, k) for k in range(1, sections)]
    other = to_other(jnp.stack(own))

    def sent_over(whole):
        return to_other(lax.dynamic_slice_in_dim(whole, (sect * 2 + 1 - core) * tokens, tokens, 0))

    def swap(block):
        return lax.all_to_all(block, ("y", "z"), 0, 0, tiled=True)

    flat = sds(256, tokens)
    sent = sds(32, 8, tokens)
    mine = pl.BlockSpec((tokens, 128), lambda i, at: (at[2], 0))
    outs = run(
        prepare_kernel,
        [sds(256, 256)] * 24,
        *own,
        other,
        at=at,
        dots=24,
        scratch=[pltpu.VMEM((4, 320, 128), BF)],
    )
    mats = [outs[6 * s : 6 * s + 6] for s in range(sections)]
    x0, z = run(
        first_kernel,
        [flat, sent],
        inputs,
        sent_over(inputs),
        mats[0][1],
        at=at,
        dots=2,
        blocks=[mine, None, None],
    )
    y = run(turn_kernel, flat, cotangent, sent_over(cotangent), at=at, blocks=[mine, None])
    z, y = lax.optimization_barrier((z, y))
    x = [x0]
    z_all, u_all = [], []
    for s in range(sections):
        z = swap(z)
        z_all.append(z)
        u = swap(run(mix_kernel, sent, z, mats[s][5]))
        u_all.append(u)
        if s + 1 < sections:
            new, z = run(gated_kernel, [flat, sent], x[s], u, mats[s][3], mats[s + 1][1], dots=2)
            x.append(new)
    last = sections - 1
    gu, gg = run(back_start_kernel, [sent, flat], y, x[last], u_all[last], mats[last][3])
    rows = sds(tokens + 320, 128)
    kept, crossed = [], []
    for s in range(last, -1, -1):
        gu = swap(gu)
        if s == 0:
            gu, kept, crossed = lax.optimization_barrier((gu, kept, crossed))
        gz = swap(run(mix_kernel, sent, gu, mats[s][4]))
        held = (x[s], gz, gg, z_all[s], gu)
        if s > 0:
            y, gu, gg = run(
                back_kernel,
                [flat, sent, flat],
                y,
                gz,
                gg,
                mats[s][0],
                mats[s][2],
                x[s - 1],
                u_all[s - 1],
                mats[s - 1][3],
                dots=3,
            )
            part, away = run(parts_kernel, [rows, rows], *held, y, at=at, dots=9)
            kept.insert(0, part)
            crossed.insert(0, to_other(away))
    joined = sds(2 * tokens + 320, 128)
    routed = run(route_kernel, [joined] * 4, *kept, *crossed, at=at)
    early = [routed[0]] + [shift(routed[k], k, (1, 2, 3)) for k in range(1, sections)]
    part, away = run(
        last_kernel, [rows, rows], *held, y, mats[0][0], mats[0][2], at=at, dots=11
    )
    final = run(join_kernel, joined, part, to_other(away), at=at)
    late = [final] + [shift(final, k, (0,)) for k in range(1, sections)]
    y_out, r_grad, g_grad, l_grad = run(
        settle_kernel,
        [
            sds(sections * 2 * tokens, 128),
            sds(128, 128, dtype=F32),
            sds(128, 128, dtype=F32),
            sds(2, 64, 64, dtype=F32),
        ],
        *early,
        *late,
        at=at,
    )
    return y_out[None], r_grad[None, None], g_grad[None, None], l_grad[None]


def solution(mesh):
    grid = Mesh(mesh.devices.reshape(4, 4, 8, 2), ("x", "y", "z", "c"))
    blk = ("y", "z", "c")
    return jax.shard_map(
        shards,
        mesh=grid,
        in_specs=(
            P(None, blk),
            P(None, blk),
            P("x", blk, None, None),
            P("x", blk, None, None),
            P("x", blk, None, None),
        ),
        out_specs=(
            P("x", None, blk),
            P("x", blk, None, None),
            P("x", blk, None, None),
            P("x", blk, None, None),
        ),
        check_vma=False,
    )
```

```python
import jax
import jax.numpy as jnp
from jax import lax
from jax.experimental import pallas as pl
from jax.experimental.pallas import tpu as pltpu
from jax.sharding import Mesh, PartitionSpec as P

BF = jnp.bfloat16
F32 = jnp.float32


def nn(a, b):
    return lax.dot_general(a, b, (((1,), (0,)), ((), ())), preferred_element_type=F32)


def nt(a, b):
    return lax.dot_general(a, b, (((1,), (1,)), ((), ())), preferred_element_type=F32)


def feature_order(rows, cols, transposed=False, offset=0):
    r = lax.broadcasted_iota(jnp.int32, (rows, cols), 1 if transposed else 0)
    c = lax.broadcasted_iota(jnp.int32, (rows, cols), 0 if transposed else 1)
    natural = ((r >> 2) & 1) * 128 + (r >> 3) * 4 + (r & 3)
    return jnp.where(natural == c + offset, 1.0, 0.0).astype(BF)


def position_order(rows, cols, transposed=False):
    r = lax.broadcasted_iota(jnp.int32, (rows, cols), 1 if transposed else 0)
    c = lax.broadcasted_iota(jnp.int32, (rows, cols), 0 if transposed else 1)
    natural = (r & 3) * 64 + (r >> 3) * 2 + ((r >> 2) & 1)
    return jnp.where(natural == c, 1.0, 0.0).astype(BF)


def rows_of(ref):
    d, i, n = ref.shape
    return ref[...].astype(F32).reshape(d * i, n)


def put_rows(ref, value):
    ref[...] = value.reshape(ref.shape).astype(ref.dtype)


def block_of(own_ref, other_ref, c, core, k, start, stop):
    mine = own_ref[k, start:stop, :].astype(F32)
    other = other_ref[k, start:stop, :].astype(F32)
    return jnp.where(core == c, mine, other)


def prepare_kernel(at_ref, *refs):
    shifted, other_ref = refs[:4], refs[4]
    outs, own_ref = refs[5:-1], refs[-1]
    sect, core = at_ref[0], at_ref[1]
    for k in range(4):
        own_ref[k] = shifted[k][...]
    p = feature_order(256, 256)
    q = position_order(256, 256)
    lane = lax.broadcasted_iota(jnp.int32, (64, 128), 1)
    for layer in range(4):
        k = lax.rem(sect - layer + 4, 4)
        r_out, rt_out, g_out, gt_out, l_out, lt_out = outs[6 * layer : 6 * layer + 6]
        for start, plain, flipped in ((0, r_out, rt_out), (128, g_out, gt_out)):
            blocks = [
                block_of(own_ref, other_ref, c, core, k, start, start + 128).astype(BF)
                for c in range(2)
            ]
            parts = [p[:, 128 * c : 128 * c + 128] for c in range(2)]
            left = jnp.concatenate([nn(parts[c], blocks[c]) for c in range(2)], axis=1).astype(BF)
            plain[...] = nt(left, p).astype(BF)
            left = jnp.concatenate([nt(parts[c], blocks[c]) for c in range(2)], axis=1).astype(BF)
            flipped[...] = nt(left, p).astype(BF)
        pairs = []
        for c in range(2):
            packed = block_of(own_ref, other_ref, c, core, k, 256, 320)
            low = jnp.where(lane < 64, packed, 0.0)
            high = jnp.where(lane < 64, 0.0, packed)
            pairs.append(jnp.concatenate([low, high], axis=0).astype(BF))
        parts = [q[:, 128 * c : 128 * c + 128] for c in range(2)]
        left = jnp.concatenate([nn(parts[c], pairs[c]) for c in range(2)], axis=1).astype(BF)
        l_out[...] = nt(left, q).astype(BF)
        left = jnp.concatenate([nt(parts[c], pairs[c]) for c in range(2)], axis=1).astype(BF)
        lt_out[...] = nt(left, q).astype(BF)


def turned(core, mine_ref, other_ref):
    p = feature_order(256, 128, offset=core * 128)
    o = feature_order(256, 128, offset=128 - core * 128)
    return (nt(p, mine_ref[...]) + nt(o, other_ref[...])).astype(BF)


def turn_kernel(at_ref, mine_ref, other_ref, o_ref):
    o_ref[...] = turned(at_ref[1], mine_ref, other_ref)


def first_kernel(at_ref, mine_ref, other_ref, rt_ref, x_ref, z_ref):
    x = turned(at_ref[1], mine_ref, other_ref)
    x_ref[...] = x
    put_rows(z_ref, nn(rt_ref[...], x))


def mix_kernel(z_ref, w_ref, u_ref):
    put_rows(u_ref, nn(w_ref[...], rows_of(z_ref).astype(BF)))


def gated_kernel(x_ref, u_ref, gt_ref, rt_ref, x_out, z_ref):
    x = x_ref[...]
    sig = jax.nn.sigmoid(nn(gt_ref[...], x))
    new = (x.astype(F32) + rows_of(u_ref) * sig).astype(BF)
    x_out[...] = new
    put_rows(z_ref, nn(rt_ref[...], new))


def gate_back(upper, x, u, gt, gu_ref, gg_ref):
    sig = jax.nn.sigmoid(nn(gt, x))
    put_rows(gu_ref, upper * sig)
    gg_ref[...] = (upper * u * sig * (1.0 - sig)).astype(BF)


def back_start_kernel(y_ref, x_ref, u_ref, gt_ref, gu_ref, gg_ref):
    gate_back(y_ref[...].astype(F32), x_ref[...], rows_of(u_ref), gt_ref[...], gu_ref, gg_ref)


def lower_of(y_ref, gz_ref, gg_ref, r_ref, g_ref):
    gz = rows_of(gz_ref).astype(BF)
    lower = y_ref[...].astype(F32) + nn(r_ref[...], gz)
    return (lower + nn(g_ref[...], gg_ref[...])).astype(BF)


def back_kernel(y_ref, gz_ref, gg_ref, r_ref, g_ref, x_ref, u_ref, gt_ref, y_out, gu_ref, gg_out):
    lower = lower_of(y_ref, gz_ref, gg_ref, r_ref, g_ref)
    y_out[...] = lower
    gate_back(lower.astype(F32), x_ref[...], rows_of(u_ref), gt_ref[...], gu_ref, gg_out)


def parts_of(x, gz, gg, z, gu, y):
    pt = feature_order(256, 256, True)
    qt = position_order(256, 256, True)
    x_n = nn(pt, x).astype(BF)
    gz_n = nn(pt, gz).astype(BF)
    gg_n = nn(pt, gg).astype(BF)
    z_n = nn(qt, z).astype(BF)
    gu_n = nn(qt, gu).astype(BF)
    y_n = nn(pt, y)
    lane = lax.broadcasted_iota(jnp.int32, (64, 128), 1)
    parts = []
    for i in range(2):
        at = slice(128 * i, 128 * i + 128)
        l_part = nt(z_n[at], gu_n[at])
        parts.append(
            (
                y_n[at].T,
                nt(x_n[at], gz_n[at]),
                nt(x_n[at], gg_n[at]),
                jnp.where(lane < 64, l_part[:64], l_part[64:]),
            )
        )
    return parts


def put_parts(core, parts, mine_out, other_out):
    start = 0
    for low, high in zip(*parts):
        stop = start + low.shape[0]
        mine_out[start:stop, :] = jnp.where(core == 0, low, high).astype(BF)
        other_out[start:stop, :] = jnp.where(core == 0, high, low).astype(BF)
        start = stop


def parts_kernel(at_ref, x_ref, gz_ref, gg_ref, z_ref, gu_ref, y_ref, mine_out, other_out):
    parts = parts_of(
        x_ref[...],
        rows_of(gz_ref).astype(BF),
        gg_ref[...],
        rows_of(z_ref).astype(BF),
        rows_of(gu_ref).astype(BF),
        y_ref[...],
    )
    put_parts(at_ref[1], parts, mine_out, other_out)


def last_kernel(
    at_ref, x_ref, gz_ref, gg_ref, z_ref, gu_ref, y_ref, r_ref, g_ref, mine_out, other_out
):
    lower = lower_of(y_ref, gz_ref, gg_ref, r_ref, g_ref)
    parts = parts_of(
        x_ref[...],
        rows_of(gz_ref).astype(BF),
        gg_ref[...],
        rows_of(z_ref).astype(BF),
        rows_of(gu_ref).astype(BF),
        lower,
    )
    put_parts(at_ref[1], parts, mine_out, other_out)


def join(core, mine_ref, other_ref, out_ref):
    n = (out_ref.shape[0] - 320) // 2
    out_ref[pl.ds(pl.multiple_of(core * n, n), n), :] = mine_ref[:n, :]
    out_ref[pl.ds(pl.multiple_of((1 - core) * n, n), n), :] = other_ref[:n, :]
    total = mine_ref[n:, :].astype(F32) + other_ref[n:, :].astype(F32)
    out_ref[2 * n :, :] = total.astype(BF)


def join_kernel(at_ref, mine_ref, other_ref, out_ref):
    join(at_ref[1], mine_ref, other_ref, out_ref)


def route_kernel(at_ref, *refs):
    sect, core = at_ref[0], at_ref[1]
    mine, other, outs = refs[:3], refs[3:6], refs[6:]
    for k in range(4):
        target = lax.rem(sect + k, 4)

        @pl.when(target == 0)
        def _():
            outs[k][...] = jnp.zeros_like(outs[k])

        for layer in range(1, 4):

            @pl.when(target == layer)
            def _():
                join(core, mine[layer - 1], other[layer - 1], outs[k])


def settle_kernel(at_ref, *refs):
    early, late = refs[:4], refs[4:8]
    y_out, r_out, g_out, l_out = refs[8:]
    sect = at_ref[0]
    n = y_out.shape[0] // 4

    def settle(parts):
        total = None
        for k in range(4):
            source = pl.multiple_of(lax.rem(sect - k + 4, 4) * n, n)
            y_out[pl.ds(source, n), :] = parts[k][:n, :]
            part = parts[k][n:, :].astype(F32)
            total = part if total is None else total + part
        r_out[...] = total[:128]
        g_out[...] = total[128:256]
        l_out[0] = total[256:, :64]
        l_out[1] = total[256:, 64:]

    @pl.when(sect == 0)
    def _():
        settle(late)

    @pl.when(sect != 0)
    def _():
        settle(early)


def run(kernel, outs, *args, dots=1, at=None, scratch=(), blocks=None):
    nbytes = sum(a.size * a.dtype.itemsize for a in args)
    params = pltpu.CompilerParams(vmem_limit_bytes=16 << 20)
    cost = pl.CostEstimate(
        flops=dots * 2 * 256 * 256 * 512, bytes_accessed=2 * nbytes, transcendentals=0
    )
    if at is None:
        return pl.pallas_call(
            kernel, out_shape=outs, compiler_params=params, cost_estimate=cost
        )(*args)
    specs = [
        spec or pl.BlockSpec(a.shape, lambda i, at, nd=a.ndim: (0,) * nd)
        for a, spec in zip(args, blocks or [None] * len(args))
    ]
    many = isinstance(outs, list)
    out_specs = [
        pl.BlockSpec(o.shape, lambda i, at, nd=len(o.shape): (0,) * nd)
        for o in (outs if many else [outs])
    ]
    return pl.pallas_call(
        kernel,
        out_shape=outs,
        grid_spec=pltpu.PrefetchScalarGridSpec(
            num_scalar_prefetch=1,
            grid=(1,),
            in_specs=specs,
            out_specs=out_specs if many else out_specs[0],
            scratch_shapes=list(scratch),
        ),
        compiler_params=params,
        cost_estimate=cost,
    )(at, *args)


def sds(*shape, dtype=BF):
    return jax.ShapeDtypeStruct(shape, dtype)


def program(inputs, cotangent, r_weight, g_weight, l_weight):
    sections = lax.axis_size("x")
    tokens = inputs.shape[0] // (sections * 2)
    sect = lax.axis_index("x")
    core = lax.axis_index("c")
    at = jnp.stack([sect, core, sect * 2 + core]).astype(jnp.int32)

    def to_other(value):
        return lax.ppermute(value, "c", [(0, 1), (1, 0)])

    def shift(value, k, targets=range(4)):
        route = [(i, (i + k) % sections) for i in range(sections)]
        return lax.ppermute(value, "x", [(i, j) for i, j in route if j in targets])

    l_flat = jnp.concatenate([l_weight[0, 0], l_weight[0, 1]], axis=1)
    packed = jnp.concatenate([r_weight[0, 0], g_weight[0, 0], l_flat], axis=0)
    own = [packed]
    for k in range(1, sections):
        own.append(shift(packed, k))
    other = to_other(jnp.stack(own))

    def sent_over(whole):
        start = (sect * 2 + 1 - core) * tokens
        return to_other(lax.dynamic_slice_in_dim(whole, start, tokens, 0))

    def swap(block):
        return lax.all_to_all(block, ("y", "z"), 0, 0, tiled=True)

    flat = sds(256, tokens)
    sent = sds(32, 8, tokens)
    mine = pl.BlockSpec((tokens, 128), lambda i, at: (at[2], 0))
    outs = run(
        prepare_kernel,
        [sds(256, 256)] * 24,
        *own,
        other,
        at=at,
        dots=24,
        scratch=[pltpu.VMEM((4, 320, 128), BF)],
    )
    mats = [outs[6 * s : 6 * s + 6] for s in range(sections)]
    x0, z = run(
        first_kernel,
        [flat, sent],
        inputs,
        sent_over(inputs),
        mats[0][1],
        at=at,
        dots=2,
        blocks=[mine, None, None],
    )
    crossed = sent_over(cotangent)
    y = run(turn_kernel, flat, cotangent, crossed, at=at, blocks=[mine, None])
    z, y = lax.optimization_barrier((z, y))
    x = [x0]
    z_all, u_all = [], []
    for s in range(sections):
        z = swap(z)
        z_all.append(z)
        u = swap(run(mix_kernel, sent, z, mats[s][5]))
        u_all.append(u)
        if s + 1 < sections:
            new, z = run(gated_kernel, [flat, sent], x[s], u, mats[s][3], mats[s + 1][1], dots=2)
            x.append(new)
    last = sections - 1
    gu, gg = run(back_start_kernel, [sent, flat], y, x[last], u_all[last], mats[last][3])
    rows = sds(tokens + 320, 128)
    joined = sds(2 * tokens + 320, 128)
    kept, crossed = [], []
    for s in range(last, -1, -1):
        gu = swap(gu)
        if s == 0:
            gu, kept, crossed = lax.optimization_barrier((gu, kept, crossed))
        mixed = run(mix_kernel, sent, gu, mats[s][4])
        if s == 0:
            routed = run(route_kernel, [joined] * 4, *kept, *crossed, at=at)
            mixed, routed = lax.optimization_barrier((mixed, routed))
        gz = swap(mixed)
        held = (x[s], gz, gg, z_all[s], gu)
        if s > 0:
            y, gu, gg = run(
                back_kernel,
                [flat, sent, flat],
                y,
                gz,
                gg,
                mats[s][0],
                mats[s][2],
                x[s - 1],
                u_all[s - 1],
                mats[s - 1][3],
                dots=3,
            )
            part, away = run(parts_kernel, [rows, rows], *held, y, at=at, dots=9)
            kept.insert(0, part)
            crossed.insert(0, to_other(away))
    early = [routed[0]]
    for k in range(1, sections):
        early.append(shift(routed[k], k, (1, 2, 3)))
    part, away = run(
        last_kernel, [rows, rows], *held, y, mats[0][0], mats[0][2], at=at, dots=11
    )
    final = run(join_kernel, joined, part, to_other(away), at=at)
    late = [final] + [shift(final, k, (0,)) for k in range(1, sections)]
    y_out, r_grad, g_grad, l_grad = run(
        settle_kernel,
        [
            sds(sections * 2 * tokens, 128),
            sds(128, 128, dtype=F32),
            sds(128, 128, dtype=F32),
            sds(2, 64, 64, dtype=F32),
        ],
        *early,
        *late,
        at=at,
    )
    return y_out[None], r_grad[None, None], g_grad[None, None], l_grad[None]


def solution(mesh):
    grid = Mesh(mesh.devices.reshape(4, 4, 8, 2), ("x", "y", "z", "c"))
    blk = ("y", "z", "c")
    return jax.shard_map(
        program,
        mesh=grid,
        in_specs=(
            P(None, blk),
            P(None, blk),
            P("x", blk, None, None),
            P("x", blk, None, None),
            P("x", blk, None, None),
        ),
        out_specs=(
            P("x", None, blk),
            P("x", blk, None, None),
            P("x", blk, None, None),
            P("x", blk, None, None),
        ),
        check_vma=False,
    )
```

```python
import jax
import jax.numpy as jnp
from jax import lax
from jax.experimental import pallas as pl
from jax.experimental.pallas import tpu as pltpu
from jax.sharding import Mesh, PartitionSpec as P

BF = jnp.bfloat16
F32 = jnp.float32


def nn(a, b):
    return lax.dot_general(a, b, (((1,), (0,)), ((), ())), preferred_element_type=F32)


def nt(a, b):
    return lax.dot_general(a, b, (((1,), (1,)), ((), ())), preferred_element_type=F32)


def feature_order(rows, cols, transposed=False, offset=0):
    r = lax.broadcasted_iota(jnp.int32, (rows, cols), 1 if transposed else 0)
    c = lax.broadcasted_iota(jnp.int32, (rows, cols), 0 if transposed else 1)
    natural = ((r >> 2) & 1) * 128 + (r >> 3) * 4 + (r & 3)
    return jnp.where(natural == c + offset, 1.0, 0.0).astype(BF)


def position_order(rows, cols, transposed=False):
    r = lax.broadcasted_iota(jnp.int32, (rows, cols), 1 if transposed else 0)
    c = lax.broadcasted_iota(jnp.int32, (rows, cols), 0 if transposed else 1)
    natural = (r & 3) * 64 + (r >> 3) * 2 + ((r >> 2) & 1)
    return jnp.where(natural == c, 1.0, 0.0).astype(BF)


def rows_of(ref, half=0):
    d, _, n = ref.shape
    return ref[:, 8 * half : 8 * half + 8, :].astype(F32).reshape(d * 8, n)


def put_rows(ref, *values):
    d, _, n = ref.shape
    slabs = [v.reshape(d, 8, n) for v in values]
    both = slabs[0] if len(slabs) == 1 else jnp.concatenate(slabs, axis=1)
    ref[...] = both.astype(ref.dtype)


def block_of(own_ref, other_ref, c, core, k, start, stop):
    mine = own_ref[k, start:stop, :].astype(F32)
    other = other_ref[k, start:stop, :].astype(F32)
    return jnp.where(core == c, mine, other)


def prepare_kernel(at_ref, *refs):
    shifted, other_ref = refs[:4], refs[4]
    outs, own_ref = refs[5:-1], refs[-1]
    sect, core = at_ref[0], at_ref[1]
    for k in range(4):
        own_ref[k] = shifted[k][...]
    p = feature_order(256, 256)
    q = position_order(256, 256)
    lane = lax.broadcasted_iota(jnp.int32, (64, 128), 1)
    for layer in range(4):
        k = lax.rem(sect - layer + 4, 4)
        r_out, rt_out, g_out, gt_out, l_out, lt_out = outs[6 * layer : 6 * layer + 6]
        for start, plain, flipped in ((0, r_out, rt_out), (128, g_out, gt_out)):
            blocks = [
                block_of(own_ref, other_ref, c, core, k, start, start + 128).astype(BF)
                for c in range(2)
            ]
            parts = [p[:, 128 * c : 128 * c + 128] for c in range(2)]
            left = jnp.concatenate([nn(parts[c], blocks[c]) for c in range(2)], axis=1).astype(BF)
            plain[...] = nt(left, p).astype(BF)
            left = jnp.concatenate([nt(parts[c], blocks[c]) for c in range(2)], axis=1).astype(BF)
            flipped[...] = nt(left, p).astype(BF)
        pairs = []
        for c in range(2):
            packed = block_of(own_ref, other_ref, c, core, k, 256, 320)
            low = jnp.where(lane < 64, packed, 0.0)
            high = jnp.where(lane < 64, 0.0, packed)
            pairs.append(jnp.concatenate([low, high], axis=0).astype(BF))
        parts = [q[:, 128 * c : 128 * c + 128] for c in range(2)]
        left = jnp.concatenate([nn(parts[c], pairs[c]) for c in range(2)], axis=1).astype(BF)
        l_out[...] = nt(left, q).astype(BF)
        left = jnp.concatenate([nt(parts[c], pairs[c]) for c in range(2)], axis=1).astype(BF)
        lt_out[...] = nt(left, q).astype(BF)


def turned(core, mine_ref, other_ref):
    p = feature_order(256, 128, offset=core * 128)
    o = feature_order(256, 128, offset=128 - core * 128)
    return (nt(p, mine_ref[...]) + nt(o, other_ref[...])).astype(BF)


def turn_kernel(at_ref, mine_ref, other_ref, o_ref):
    o_ref[...] = turned(at_ref[1], mine_ref, other_ref)


def first_kernel(at_ref, mine_ref, other_ref, rt_ref, x_ref, z_ref):
    x = turned(at_ref[1], mine_ref, other_ref)
    x_ref[...] = x
    put_rows(z_ref, nn(rt_ref[...], x))


def mix_kernel(z_ref, w_ref, u_ref):
    put_rows(u_ref, nn(w_ref[...], rows_of(z_ref).astype(BF)))


def gated_kernel(x_ref, u_ref, gt_ref, rt_ref, x_out, z_ref):
    x = x_ref[...]
    sig = jax.nn.sigmoid(nn(gt_ref[...], x))
    new = (x.astype(F32) + rows_of(u_ref) * sig).astype(BF)
    x_out[...] = new
    put_rows(z_ref, nn(rt_ref[...], new))


def mix_both_kernel(pair_ref, lt_ref, l_ref, out_ref):
    u = nn(lt_ref[...], rows_of(pair_ref, 0).astype(BF))
    gz = nn(l_ref[...], rows_of(pair_ref, 1).astype(BF))
    put_rows(out_ref, u, gz)


def top_kernel(x_ref, u_ref, gt_ref, rt_ref, y_ref, gt_top_ref, x_out, pair_ref):
    x = x_ref[...]
    sig = jax.nn.sigmoid(nn(gt_ref[...], x))
    new = (x.astype(F32) + rows_of(u_ref) * sig).astype(BF)
    x_out[...] = new
    top = jax.nn.sigmoid(nn(gt_top_ref[...], new))
    put_rows(pair_ref, nn(rt_ref[...], new), y_ref[...].astype(F32) * top)


def gate_back(upper, x, u, gt, gu_ref, gg_ref):
    sig = jax.nn.sigmoid(nn(gt, x))
    put_rows(gu_ref, upper * sig)
    gg_ref[...] = (upper * u * sig * (1.0 - sig)).astype(BF)


def lower_of(y, gz, gg, r, g):
    return (y.astype(F32) + nn(r, gz) + nn(g, gg)).astype(BF)


def top_back_kernel(
    y_ref, pair_ref, x_top_ref, gt_top_ref, r_ref, g_ref, x_ref, u_ref, gt_ref, y_out, gg_top_out, gu_ref, gg_out
):
    y = y_ref[...]
    sig = jax.nn.sigmoid(nn(gt_top_ref[...], x_top_ref[...]))
    gg = (y.astype(F32) * rows_of(pair_ref, 0) * sig * (1.0 - sig)).astype(BF)
    gg_top_out[...] = gg
    lower = lower_of(y, rows_of(pair_ref, 1).astype(BF), gg, r_ref[...], g_ref[...])
    y_out[...] = lower
    gate_back(lower.astype(F32), x_ref[...], rows_of(u_ref), gt_ref[...], gu_ref, gg_out)


def back_kernel(y_ref, gz_ref, gg_ref, r_ref, g_ref, x_ref, u_ref, gt_ref, y_out, gu_ref, gg_out):
    gz = rows_of(gz_ref).astype(BF)
    lower = lower_of(y_ref[...], gz, gg_ref[...], r_ref[...], g_ref[...])
    y_out[...] = lower
    gate_back(lower.astype(F32), x_ref[...], rows_of(u_ref), gt_ref[...], gu_ref, gg_out)


def parts_of(x, gz, gg, z, gu, y):
    pt = feature_order(256, 256, True)
    qt = position_order(256, 256, True)
    x_n = nn(pt, x).astype(BF)
    gz_n = nn(pt, gz).astype(BF)
    gg_n = nn(pt, gg).astype(BF)
    z_n = nn(qt, z).astype(BF)
    gu_n = nn(qt, gu).astype(BF)
    y_n = nn(pt, y)
    lane = lax.broadcasted_iota(jnp.int32, (64, 128), 1)
    parts = []
    for i in range(2):
        at = slice(128 * i, 128 * i + 128)
        l_part = nt(z_n[at], gu_n[at])
        parts.append(
            (
                y_n[at].T,
                nt(x_n[at], gz_n[at]),
                nt(x_n[at], gg_n[at]),
                jnp.where(lane < 64, l_part[:64], l_part[64:]),
            )
        )
    return parts


def put_parts(parts, out_ref):
    for c in range(2):
        start = 0
        for part in parts[c]:
            stop = start + part.shape[0]
            out_ref[0, c, start:stop, :] = part.astype(BF)
            start = stop


def top_parts_kernel(x_ref, gave_ref, gg_ref, took_ref, y_ref, out_ref):
    gz = rows_of(gave_ref, 1).astype(BF)
    z = rows_of(took_ref, 0).astype(BF)
    gu = rows_of(took_ref, 1).astype(BF)
    put_parts(parts_of(x_ref[...], gz, gg_ref[...], z, gu, y_ref[...]), out_ref)


def parts_kernel(x_ref, gz_ref, gg_ref, z_ref, gu_ref, y_ref, held_ref, out_ref):
    gz = rows_of(gz_ref).astype(BF)
    z = rows_of(z_ref).astype(BF)
    gu = rows_of(gu_ref).astype(BF)
    put_parts(parts_of(x_ref[...], gz, gg_ref[...], z, gu, y_ref[...]), out_ref)


def last_kernel(x_ref, gz_ref, gg_ref, z_ref, gu_ref, y_ref, r_ref, g_ref, held_ref, out_ref):
    gz = rows_of(gz_ref).astype(BF)
    z = rows_of(z_ref).astype(BF)
    gu = rows_of(gu_ref).astype(BF)
    lower = lower_of(y_ref[...], gz, gg_ref[...], r_ref[...], g_ref[...])
    put_parts(parts_of(x_ref[...], gz, gg_ref[...], z, gu, lower), out_ref)


def settle_kernel(got_ref, y_out, r_out, g_out, l_out):
    n = y_out.shape[0] // 8
    total = None
    for i in range(8):
        y_out[n * i : n * i + n, :] = got_ref[i, :n, :]
        part = got_ref[i, n:, :].astype(F32)
        total = part if total is None else total + part
    r_out[...] = total[:128]
    g_out[...] = total[128:256]
    l_out[0] = total[256:, :64]
    l_out[1] = total[256:, 64:]


def run(kernel, outs, *args, dots=1, at=None, scratch=(), blocks=None):
    nbytes = sum(a.size * a.dtype.itemsize for a in args)
    params = pltpu.CompilerParams(vmem_limit_bytes=16 << 20)
    cost = pl.CostEstimate(
        flops=dots * 2 * 256 * 256 * 512, bytes_accessed=2 * nbytes, transcendentals=0
    )
    if at is None:
        return pl.pallas_call(
            kernel, out_shape=outs, compiler_params=params, cost_estimate=cost
        )(*args)
    specs = [
        spec or pl.BlockSpec(a.shape, lambda i, at, nd=a.ndim: (0,) * nd)
        for a, spec in zip(args, blocks or [None] * len(args))
    ]
    many = isinstance(outs, list)
    out_specs = [
        pl.BlockSpec(o.shape, lambda i, at, nd=len(o.shape): (0,) * nd)
        for o in (outs if many else [outs])
    ]
    return pl.pallas_call(
        kernel,
        out_shape=outs,
        grid_spec=pltpu.PrefetchScalarGridSpec(
            num_scalar_prefetch=1,
            grid=(1,),
            in_specs=specs,
            out_specs=out_specs if many else out_specs[0],
            scratch_shapes=list(scratch),
        ),
        compiler_params=params,
        cost_estimate=cost,
    )(at, *args)


def run_parts(kernel, layer, whole, *args):
    more = {} if layer == 3 else {"input_output_aliases": {len(args) - 1: 0}}
    specs = [pl.BlockSpec(a.shape, lambda i, nd=a.ndim: (0,) * nd) for a in args]
    if layer != 3:
        specs[-1] = pl.BlockSpec(memory_space=pl.ANY)
    return pl.pallas_call(
        kernel,
        out_shape=whole,
        grid=(1,),
        in_specs=specs,
        out_specs=pl.BlockSpec((1,) + whole.shape[1:], lambda i: (layer, 0, 0, 0)),
        compiler_params=pltpu.CompilerParams(vmem_limit_bytes=16 << 20),
        cost_estimate=pl.CostEstimate(
            flops=18 * 256 * 256 * 512, bytes_accessed=3 << 20, transcendentals=0
        ),
        **more,
    )(*args)


def sds(*shape, dtype=BF):
    return jax.ShapeDtypeStruct(shape, dtype)


def program(inputs, cotangent, r_weight, g_weight, l_weight):
    sections = lax.axis_size("x")
    tokens = inputs.shape[0] // (sections * 2)
    sect = lax.axis_index("x")
    core = lax.axis_index("c")
    at = jnp.stack([sect, core, sect * 2 + core]).astype(jnp.int32)

    def to_other(value):
        return lax.ppermute(value, "c", [(0, 1), (1, 0)])

    def shift(value, k):
        return lax.ppermute(value, "x", [(i, (i + k) % sections) for i in range(sections)])

    l_flat = jnp.concatenate([l_weight[0, 0], l_weight[0, 1]], axis=1)
    packed = jnp.concatenate([r_weight[0, 0], g_weight[0, 0], l_flat], axis=0)
    own = [packed]
    for k in range(1, sections):
        own.append(shift(packed, k))
    other = to_other(jnp.stack(own))

    def sent_over(whole):
        start = (sect * 2 + 1 - core) * tokens
        return to_other(lax.dynamic_slice_in_dim(whole, start, tokens, 0))

    def swap(block):
        return lax.all_to_all(block, ("y", "z"), 0, 0, tiled=True)

    flat = sds(256, tokens)
    sent = sds(32, 8, tokens)
    mine = pl.BlockSpec((tokens, 128), lambda i, at: (at[2], 0))
    outs = run(
        prepare_kernel,
        [sds(256, 256)] * 24,
        *own,
        other,
        at=at,
        dots=24,
        scratch=[pltpu.VMEM((4, 320, 128), BF)],
    )
    mats = [outs[6 * s : 6 * s + 6] for s in range(sections)]
    x0, z = run(
        first_kernel,
        [flat, sent],
        inputs,
        sent_over(inputs),
        mats[0][1],
        at=at,
        dots=2,
        blocks=[mine, None, None],
    )
    crossed = sent_over(cotangent)
    y = run(turn_kernel, flat, cotangent, crossed, at=at, blocks=[mine, None])
    z, y = lax.optimization_barrier((z, y))
    x = [x0]
    z_all, u_all = [], []
    last = sections - 1
    pair = sds(32, 16, tokens)
    for s in range(last):
        z = swap(z)
        z_all.append(z)
        u = swap(run(mix_kernel, sent, z, mats[s][5]))
        u_all.append(u)
        if s + 1 < last:
            new, z = run(gated_kernel, [flat, sent], x[s], u, mats[s][3], mats[s + 1][1], dots=2)
        else:
            new, both = run(
                top_kernel,
                [flat, pair],
                x[s],
                u,
                mats[s][3],
                mats[last][1],
                y,
                mats[last][3],
                dots=3,
            )
        x.append(new)
    took = swap(both)
    gave = swap(run(mix_both_kernel, pair, took, mats[last][5], mats[last][4], dots=2))
    y, gg_top, gu, gg = run(
        top_back_kernel,
        [flat, flat, sent, flat],
        y,
        gave,
        x[last],
        mats[last][3],
        mats[last][0],
        mats[last][2],
        x[last - 1],
        u_all[last - 1],
        mats[last - 1][3],
        dots=4,
    )
    whole = sds(sections, 2, tokens + 320, 128)
    parts = run_parts(top_parts_kernel, last, whole, x[last], gave, gg_top, took, y)
    for s in range(last - 1, -1, -1):
        gu = swap(gu)
        gz = swap(run(mix_kernel, sent, gu, mats[s][4]))
        held = (x[s], gz, gg, z_all[s], gu)
        if s > 0:
            y, gu, gg = run(
                back_kernel,
                [flat, sent, flat],
                y,
                gz,
                gg,
                mats[s][0],
                mats[s][2],
                x[s - 1],
                u_all[s - 1],
                mats[s - 1][3],
                dots=3,
            )
            parts = run_parts(parts_kernel, s, whole, *held, y, parts)
    parts = run_parts(last_kernel, 0, whole, *held, y, mats[0][0], mats[0][2], parts)
    got = lax.all_to_all(
        parts.reshape(sections * 2, tokens + 320, 128), ("x", "c"), 0, 0, tiled=True
    )
    y_out, r_grad, g_grad, l_grad = run(
        settle_kernel,
        [
            sds(sections * 2 * tokens, 128),
            sds(128, 128, dtype=F32),
            sds(128, 128, dtype=F32),
            sds(2, 64, 64, dtype=F32),
        ],
        got,
    )
    return y_out[None], r_grad[None, None], g_grad[None, None], l_grad[None]


def solution(mesh):
    grid = Mesh(mesh.devices.reshape(4, 4, 8, 2), ("x", "y", "z", "c"))
    blk = ("y", "z", "c")
    return jax.shard_map(
        program,
        mesh=grid,
        in_specs=(
            P(None, blk),
            P(None, blk),
            P("x", blk, None, None),
            P("x", blk, None, None),
            P("x", blk, None, None),
        ),
        out_specs=(
            P("x", None, blk),
            P("x", blk, None, None),
            P("x", blk, None, None),
            P("x", blk, None, None),
        ),
        check_vma=False,
    )
```

```python
import jax
import jax.numpy as jnp
from jax import lax
from jax.experimental import pallas as pl
from jax.experimental.pallas import tpu as pltpu
from jax.sharding import Mesh, PartitionSpec as P

BF = jnp.bfloat16
F32 = jnp.float32


def nn(a, b):
    return lax.dot_general(a, b, (((1,), (0,)), ((), ())), preferred_element_type=F32)


def nt(a, b):
    return lax.dot_general(a, b, (((1,), (1,)), ((), ())), preferred_element_type=F32)


def feature_order(rows, cols, transposed=False, offset=0):
    r = lax.broadcasted_iota(jnp.int32, (rows, cols), 1 if transposed else 0)
    c = lax.broadcasted_iota(jnp.int32, (rows, cols), 0 if transposed else 1)
    natural = ((r >> 2) & 1) * 128 + (r >> 3) * 4 + (r & 3)
    return jnp.where(natural == c + offset, 1.0, 0.0).astype(BF)


def position_order(rows, cols, transposed=False):
    r = lax.broadcasted_iota(jnp.int32, (rows, cols), 1 if transposed else 0)
    c = lax.broadcasted_iota(jnp.int32, (rows, cols), 0 if transposed else 1)
    natural = (r & 3) * 64 + (r >> 3) * 2 + ((r >> 2) & 1)
    return jnp.where(natural == c, 1.0, 0.0).astype(BF)


def rows_of(ref, half=0):
    d, _, n = ref.shape
    return ref[:, 8 * half : 8 * half + 8, :].astype(F32).reshape(d * 8, n)


def put_rows(ref, *values):
    d, _, n = ref.shape
    slabs = [v.reshape(d, 8, n) for v in values]
    both = slabs[0] if len(slabs) == 1 else jnp.concatenate(slabs, axis=1)
    ref[...] = both.astype(ref.dtype)


def block_of(own_ref, other_ref, c, core, k, start, stop):
    mine = own_ref[k, start:stop, :].astype(F32)
    other = other_ref[k, start:stop, :].astype(F32)
    return jnp.where(core == c, mine, other)


def prepare_kernel(at_ref, *refs):
    shifted, other_ref = refs[:4], refs[4]
    outs, own_ref = refs[5:-1], refs[-1]
    sect, core = at_ref[0], at_ref[1]
    for k in range(4):
        own_ref[k] = shifted[k][...]
    p = feature_order(256, 256)
    q = position_order(256, 256)
    lane = lax.broadcasted_iota(jnp.int32, (64, 128), 1)
    for layer in range(4):
        k = lax.rem(sect - layer + 4, 4)
        r_out, rt_out, g_out, gt_out, l_out, lt_out = outs[6 * layer : 6 * layer + 6]
        for start, plain, flipped in ((0, r_out, rt_out), (128, g_out, gt_out)):
            blocks = [
                block_of(own_ref, other_ref, c, core, k, start, start + 128).astype(BF)
                for c in range(2)
            ]
            parts = [p[:, 128 * c : 128 * c + 128] for c in range(2)]
            left = jnp.concatenate([nn(parts[c], blocks[c]) for c in range(2)], axis=1).astype(BF)
            plain[...] = nt(left, p).astype(BF)
            left = jnp.concatenate([nt(parts[c], blocks[c]) for c in range(2)], axis=1).astype(BF)
            flipped[...] = nt(left, p).astype(BF)
        pairs = []
        for c in range(2):
            packed = block_of(own_ref, other_ref, c, core, k, 256, 320)
            low = jnp.where(lane < 64, packed, 0.0)
            high = jnp.where(lane < 64, 0.0, packed)
            pairs.append(jnp.concatenate([low, high], axis=0).astype(BF))
        parts = [q[:, 128 * c : 128 * c + 128] for c in range(2)]
        left = jnp.concatenate([nn(parts[c], pairs[c]) for c in range(2)], axis=1).astype(BF)
        l_out[...] = nt(left, q).astype(BF)
        left = jnp.concatenate([nt(parts[c], pairs[c]) for c in range(2)], axis=1).astype(BF)
        lt_out[...] = nt(left, q).astype(BF)


def turned(core, mine_ref, other_ref):
    p = feature_order(256, 128, offset=core * 128)
    o = feature_order(256, 128, offset=128 - core * 128)
    return (nt(p, mine_ref[...]) + nt(o, other_ref[...])).astype(BF)


def first_kernel(at_ref, mine_ref, other_ref, rt_ref, x_ref, z_ref):
    x = turned(at_ref[1], mine_ref, other_ref)
    x_ref[...] = x
    put_rows(z_ref, nn(rt_ref[...], x))


def mix_kernel(z_ref, w_ref, u_ref):
    put_rows(u_ref, nn(w_ref[...], rows_of(z_ref).astype(BF)))


def gated_kernel(x_ref, u_ref, gt_ref, rt_ref, x_out, z_ref):
    x = x_ref[...]
    sig = jax.nn.sigmoid(nn(gt_ref[...], x))
    new = (x.astype(F32) + rows_of(u_ref) * sig).astype(BF)
    x_out[...] = new
    put_rows(z_ref, nn(rt_ref[...], new))


def mix_both_kernel(pair_ref, lt_ref, l_ref, out_ref):
    u = nn(lt_ref[...], rows_of(pair_ref, 0).astype(BF))
    gz = nn(l_ref[...], rows_of(pair_ref, 1).astype(BF))
    put_rows(out_ref, u, gz)


def top_kernel(
    at_ref, x_ref, u_ref, gt_ref, rt_ref, mine_ref, other_ref, gt_top_ref, x_out, pair_ref, y_out
):
    x = x_ref[...]
    sig = jax.nn.sigmoid(nn(gt_ref[...], x))
    new = (x.astype(F32) + rows_of(u_ref) * sig).astype(BF)
    x_out[...] = new
    top = jax.nn.sigmoid(nn(gt_top_ref[...], new))
    y = turned(at_ref[1], mine_ref, other_ref)
    y_out[...] = y
    put_rows(pair_ref, nn(rt_ref[...], new), y.astype(F32) * top)


def gate_back(upper, x, u, gt, gu_ref, gg_ref):
    sig = jax.nn.sigmoid(nn(gt, x))
    put_rows(gu_ref, upper * sig)
    gg_ref[...] = (upper * u * sig * (1.0 - sig)).astype(BF)


def lower_of(y, gz, gg, r, g):
    return (y.astype(F32) + nn(r, gz) + nn(g, gg)).astype(BF)


def top_back_kernel(
    y_ref, pair_ref, x_top_ref, gt_top_ref, r_ref, g_ref, x_ref, u_ref, gt_ref, y_out, gg_top_out, gu_ref, gg_out
):
    y = y_ref[...]
    sig = jax.nn.sigmoid(nn(gt_top_ref[...], x_top_ref[...]))
    gg = (y.astype(F32) * rows_of(pair_ref, 0) * sig * (1.0 - sig)).astype(BF)
    gg_top_out[...] = gg
    lower = lower_of(y, rows_of(pair_ref, 1).astype(BF), gg, r_ref[...], g_ref[...])
    y_out[...] = lower
    gate_back(lower.astype(F32), x_ref[...], rows_of(u_ref), gt_ref[...], gu_ref, gg_out)


def back_kernel(y_ref, gz_ref, gg_ref, r_ref, g_ref, x_ref, u_ref, gt_ref, y_out, gu_ref, gg_out):
    gz = rows_of(gz_ref).astype(BF)
    lower = lower_of(y_ref[...], gz, gg_ref[...], r_ref[...], g_ref[...])
    y_out[...] = lower
    gate_back(lower.astype(F32), x_ref[...], rows_of(u_ref), gt_ref[...], gu_ref, gg_out)


def parts_of(x, gz, gg, z, gu, y):
    pt = feature_order(256, 256, True)
    qt = position_order(256, 256, True)
    x_n = nn(pt, x).astype(BF)
    gz_n = nn(pt, gz).astype(BF)
    gg_n = nn(pt, gg).astype(BF)
    z_n = nn(qt, z).astype(BF)
    gu_n = nn(qt, gu).astype(BF)
    y_n = nn(pt, y)
    lane = lax.broadcasted_iota(jnp.int32, (64, 128), 1)
    parts = []
    for i in range(2):
        at = slice(128 * i, 128 * i + 128)
        l_part = nt(z_n[at], gu_n[at])
        parts.append(
            (
                y_n[at].T,
                nt(x_n[at], gz_n[at]),
                nt(x_n[at], gg_n[at]),
                jnp.where(lane < 64, l_part[:64], l_part[64:]),
            )
        )
    return parts


def put_parts(parts, out_ref):
    for c in range(2):
        start = 0
        for part in parts[c]:
            stop = start + part.shape[0]
            out_ref[0, c, start:stop, :] = part.astype(BF)
            start = stop


def top_parts_kernel(x_ref, gave_ref, gg_ref, took_ref, y_ref, out_ref):
    gz = rows_of(gave_ref, 1).astype(BF)
    z = rows_of(took_ref, 0).astype(BF)
    gu = rows_of(took_ref, 1).astype(BF)
    put_parts(parts_of(x_ref[...], gz, gg_ref[...], z, gu, y_ref[...]), out_ref)


def parts_kernel(x_ref, gz_ref, gg_ref, z_ref, gu_ref, y_ref, held_ref, out_ref):
    gz = rows_of(gz_ref).astype(BF)
    z = rows_of(z_ref).astype(BF)
    gu = rows_of(gu_ref).astype(BF)
    put_parts(parts_of(x_ref[...], gz, gg_ref[...], z, gu, y_ref[...]), out_ref)


def last_kernel(x_ref, gz_ref, gg_ref, z_ref, gu_ref, y_ref, r_ref, g_ref, held_ref, out_ref):
    gz = rows_of(gz_ref).astype(BF)
    z = rows_of(z_ref).astype(BF)
    gu = rows_of(gu_ref).astype(BF)
    lower = lower_of(y_ref[...], gz, gg_ref[...], r_ref[...], g_ref[...])
    put_parts(parts_of(x_ref[...], gz, gg_ref[...], z, gu, lower), out_ref)


def settle_kernel(got_ref, y_out, r_out, g_out, l_out):
    n = y_out.shape[0] // 8
    total = None
    for i in range(8):
        y_out[n * i : n * i + n, :] = got_ref[i, :n, :]
        part = got_ref[i, n:, :].astype(F32)
        total = part if total is None else total + part
    r_out[...] = total[:128]
    g_out[...] = total[128:256]
    l_out[0] = total[256:, :64]
    l_out[1] = total[256:, 64:]


def run(kernel, outs, *args, dots=1, at=None, scratch=(), blocks=None):
    nbytes = sum(a.size * a.dtype.itemsize for a in args)
    params = pltpu.CompilerParams(vmem_limit_bytes=16 << 20)
    cost = pl.CostEstimate(
        flops=dots * 2 * 256 * 256 * 512, bytes_accessed=2 * nbytes, transcendentals=0
    )
    if at is None:
        return pl.pallas_call(
            kernel, out_shape=outs, compiler_params=params, cost_estimate=cost
        )(*args)
    specs = [
        spec or pl.BlockSpec(a.shape, lambda i, at, nd=a.ndim: (0,) * nd)
        for a, spec in zip(args, blocks or [None] * len(args))
    ]
    many = isinstance(outs, list)
    out_specs = [
        pl.BlockSpec(o.shape, lambda i, at, nd=len(o.shape): (0,) * nd)
        for o in (outs if many else [outs])
    ]
    return pl.pallas_call(
        kernel,
        out_shape=outs,
        grid_spec=pltpu.PrefetchScalarGridSpec(
            num_scalar_prefetch=1,
            grid=(1,),
            in_specs=specs,
            out_specs=out_specs if many else out_specs[0],
            scratch_shapes=list(scratch),
        ),
        compiler_params=params,
        cost_estimate=cost,
    )(at, *args)


def run_parts(kernel, layer, whole, *args):
    more = {} if layer == 3 else {"input_output_aliases": {len(args) - 1: 0}}
    specs = [pl.BlockSpec(a.shape, lambda i, nd=a.ndim: (0,) * nd) for a in args]
    if layer != 3:
        specs[-1] = pl.BlockSpec(memory_space=pl.ANY)
    return pl.pallas_call(
        kernel,
        out_shape=whole,
        grid=(1,),
        in_specs=specs,
        out_specs=pl.BlockSpec((1,) + whole.shape[1:], lambda i: (layer, 0, 0, 0)),
        compiler_params=pltpu.CompilerParams(vmem_limit_bytes=16 << 20),
        cost_estimate=pl.CostEstimate(
            flops=18 * 256 * 256 * 512, bytes_accessed=3 << 20, transcendentals=0
        ),
        **more,
    )(*args)


def sds(*shape, dtype=BF):
    return jax.ShapeDtypeStruct(shape, dtype)


def program(inputs, cotangent, r_weight, g_weight, l_weight):
    sections = lax.axis_size("x")
    tokens = inputs.shape[0] // (sections * 2)
    sect = lax.axis_index("x")
    core = lax.axis_index("c")
    at = jnp.stack([sect, core, sect * 2 + core]).astype(jnp.int32)

    def to_other(value):
        return lax.ppermute(value, "c", [(0, 1), (1, 0)])

    def shift(value, k):
        return lax.ppermute(value, "x", [(i, (i + k) % sections) for i in range(sections)])

    l_flat = jnp.concatenate([l_weight[0, 0], l_weight[0, 1]], axis=1)
    packed = jnp.concatenate([r_weight[0, 0], g_weight[0, 0], l_flat], axis=0)
    own = [packed]
    for k in range(1, sections):
        own.append(shift(packed, k))
    other = to_other(jnp.stack(own))

    def sent_over(whole):
        start = (sect * 2 + 1 - core) * tokens
        return to_other(lax.dynamic_slice_in_dim(whole, start, tokens, 0))

    def swap(block):
        return lax.all_to_all(block, ("y", "z"), 0, 0, tiled=True)

    flat = sds(256, tokens)
    sent = sds(32, 8, tokens)
    mine = pl.BlockSpec((tokens, 128), lambda i, at: (at[2], 0))
    outs = run(
        prepare_kernel,
        [sds(256, 256)] * 24,
        *own,
        other,
        at=at,
        dots=24,
        scratch=[pltpu.VMEM((4, 320, 128), BF)],
    )
    mats = [outs[6 * s : 6 * s + 6] for s in range(sections)]
    x0, z = run(
        first_kernel,
        [flat, sent],
        inputs,
        sent_over(inputs),
        mats[0][1],
        at=at,
        dots=2,
        blocks=[mine, None, None],
    )
    crossed = sent_over(cotangent)
    z, crossed = lax.optimization_barrier((z, crossed))
    x = [x0]
    z_all, u_all = [], []
    last = sections - 1
    pair = sds(32, 16, tokens)
    for s in range(last):
        z = swap(z)
        z_all.append(z)
        u = swap(run(mix_kernel, sent, z, mats[s][5]))
        u_all.append(u)
        if s + 1 < last:
            new, z = run(gated_kernel, [flat, sent], x[s], u, mats[s][3], mats[s + 1][1], dots=2)
        else:
            new, both, y = run(
                top_kernel,
                [flat, pair, flat],
                x[s],
                u,
                mats[s][3],
                mats[last][1],
                cotangent,
                crossed,
                mats[last][3],
                dots=4,
                at=at,
                blocks=[None, None, None, None, mine, None, None],
            )
        x.append(new)
    took = swap(both)
    gave = swap(run(mix_both_kernel, pair, took, mats[last][5], mats[last][4], dots=2))
    y, gg_top, gu, gg = run(
        top_back_kernel,
        [flat, flat, sent, flat],
        y,
        gave,
        x[last],
        mats[last][3],
        mats[last][0],
        mats[last][2],
        x[last - 1],
        u_all[last - 1],
        mats[last - 1][3],
        dots=4,
    )
    whole = sds(sections, 2, tokens + 320, 128)
    parts = run_parts(top_parts_kernel, last, whole, x[last], gave, gg_top, took, y)
    for s in range(last - 1, -1, -1):
        gu, parts = lax.optimization_barrier((gu, parts))
        gu = swap(gu)
        gz = swap(run(mix_kernel, sent, gu, mats[s][4]))
        held = (x[s], gz, gg, z_all[s], gu)
        if s > 0:
            y, gu, gg = run(
                back_kernel,
                [flat, sent, flat],
                y,
                gz,
                gg,
                mats[s][0],
                mats[s][2],
                x[s - 1],
                u_all[s - 1],
                mats[s - 1][3],
                dots=3,
            )
            parts = run_parts(parts_kernel, s, whole, *held, y, parts)
    parts = run_parts(last_kernel, 0, whole, *held, y, mats[0][0], mats[0][2], parts)
    got = lax.all_to_all(
        parts.reshape(sections * 2, tokens + 320, 128), ("x", "c"), 0, 0, tiled=True
    )
    y_out, r_grad, g_grad, l_grad = run(
        settle_kernel,
        [
            sds(sections * 2 * tokens, 128),
            sds(128, 128, dtype=F32),
            sds(128, 128, dtype=F32),
            sds(2, 64, 64, dtype=F32),
        ],
        got,
    )
    return y_out[None], r_grad[None, None], g_grad[None, None], l_grad[None]


def solution(mesh):
    grid = Mesh(mesh.devices.reshape(4, 4, 8, 2), ("x", "y", "z", "c"))
    blk = ("y", "z", "c")
    return jax.shard_map(
        program,
        mesh=grid,
        in_specs=(
            P(None, blk),
            P(None, blk),
            P("x", blk, None, None),
            P("x", blk, None, None),
            P("x", blk, None, None),
        ),
        out_specs=(
            P("x", None, blk),
            P("x", blk, None, None),
            P("x", blk, None, None),
            P("x", blk, None, None),
        ),
        check_vma=False,
    )
```

```python
import jax
import jax.numpy as jnp
from jax import lax
from jax.experimental import pallas as pl
from jax.experimental.pallas import tpu as pltpu
from jax.sharding import Mesh, PartitionSpec as P

BF = jnp.bfloat16
F32 = jnp.float32


def nn(a, b):
    return lax.dot_general(a, b, (((1,), (0,)), ((), ())), preferred_element_type=F32)


def nt(a, b):
    return lax.dot_general(a, b, (((1,), (1,)), ((), ())), preferred_element_type=F32)


def feature_order(rows, cols, transposed=False, offset=0):
    r = lax.broadcasted_iota(jnp.int32, (rows, cols), 1 if transposed else 0)
    c = lax.broadcasted_iota(jnp.int32, (rows, cols), 0 if transposed else 1)
    natural = ((r >> 2) & 1) * 128 + (r >> 3) * 4 + (r & 3)
    return jnp.where(natural == c + offset, 1.0, 0.0).astype(BF)


def position_order(rows, cols, transposed=False):
    r = lax.broadcasted_iota(jnp.int32, (rows, cols), 1 if transposed else 0)
    c = lax.broadcasted_iota(jnp.int32, (rows, cols), 0 if transposed else 1)
    natural = (r & 3) * 64 + (r >> 3) * 2 + ((r >> 2) & 1)
    return jnp.where(natural == c, 1.0, 0.0).astype(BF)


def rows_of(ref, half=0):
    d, _, n = ref.shape
    return ref[:, 8 * half : 8 * half + 8, :].astype(F32).reshape(d * 8, n)


def put_rows(ref, *values):
    d, _, n = ref.shape
    slabs = [v.reshape(d, 8, n) for v in values]
    both = slabs[0] if len(slabs) == 1 else jnp.concatenate(slabs, axis=1)
    ref[...] = both.astype(ref.dtype)


def block_of(own_ref, other_ref, c, core, k, start, stop):
    mine = own_ref[k, start:stop, :].astype(F32)
    other = other_ref[k, start:stop, :].astype(F32)
    return jnp.where(core == c, mine, other)


def pack_kernel(r_ref, g_ref, l_ref, out_ref, pair_ref, sems):
    copies = [
        pltpu.make_async_copy(r_ref.at[0, 0], out_ref.at[pl.ds(0, 128)], sems.at[0]),
        pltpu.make_async_copy(g_ref.at[0, 0], out_ref.at[pl.ds(128, 128)], sems.at[1]),
        pltpu.make_async_copy(l_ref.at[0], pair_ref, sems.at[2]),
    ]
    for copy in copies:
        copy.start()
    for copy in copies:
        copy.wait()
    both = [pair_ref[i].astype(F32) for i in range(2)]
    out_ref[256:320, :] = jnp.concatenate(both, axis=1).astype(BF)


def prepare_kernel(at_ref, own_ref, other_ref, *refs):
    outs, wide_ref = refs[:-1], refs[-1]
    sect, core = at_ref[0], at_ref[1]
    p = feature_order(256, 256)
    q = position_order(256, 256)
    lane = lax.broadcasted_iota(jnp.int32, (64, 128), 1)
    wide_ref[...] = jnp.zeros_like(wide_ref)
    for layer in range(4):
        apart = layer ^ sect
        k = apart ^ (apart >> 1)
        outs_of = outs[6 * layer : 6 * layer + 6]
        for i, start in enumerate((0, 128, 256)):
            order = p if i < 2 else q
            for c in range(2):
                block = block_of(own_ref, other_ref, c, core, k, start, min(start + 128, 320))
                if i == 2:
                    low = jnp.where(lane < 64, block, 0.0)
                    high = jnp.where(lane < 64, 0.0, block)
                    block = jnp.concatenate([low, high], axis=0)
                at = slice(128 * c, 128 * c + 128)
                wide_ref[i, at, at] = block.astype(BF)
            wide = wide_ref[i]
            outs_of[2 * i][...] = nt(nn(order, wide).astype(BF), order).astype(BF)
            outs_of[2 * i + 1][...] = nt(nt(order, wide).astype(BF), order).astype(BF)


def turned(core, mine_ref, other_ref):
    p = feature_order(256, 128, offset=core * 128)
    o = feature_order(256, 128, offset=128 - core * 128)
    return (nt(p, mine_ref[...]) + nt(o, other_ref[...])).astype(BF)


def turn_kernel(at_ref, mine_ref, other_ref, x_ref):
    x_ref[...] = turned(at_ref[1], mine_ref, other_ref)


def first_kernel(x_ref, rt_ref, z_ref):
    put_rows(z_ref, nn(rt_ref[...], x_ref[...]))


def mix_kernel(z_ref, w_ref, u_ref):
    put_rows(u_ref, nn(w_ref[...], rows_of(z_ref).astype(BF)))


def gated_kernel(x_ref, u_ref, gt_ref, rt_ref, x_out, z_ref):
    x = x_ref[...]
    sig = jax.nn.sigmoid(nn(gt_ref[...], x))
    new = (x.astype(F32) + rows_of(u_ref) * sig).astype(BF)
    x_out[...] = new
    put_rows(z_ref, nn(rt_ref[...], new))


def mix_both_kernel(pair_ref, lt_ref, l_ref, out_ref):
    u = nn(lt_ref[...], rows_of(pair_ref, 0).astype(BF))
    gz = nn(l_ref[...], rows_of(pair_ref, 1).astype(BF))
    put_rows(out_ref, u, gz)


def top_kernel(
    at_ref, x_ref, u_ref, gt_ref, rt_ref, mine_ref, other_ref, gt_top_ref, x_out, pair_ref, y_out
):
    x = x_ref[...]
    sig = jax.nn.sigmoid(nn(gt_ref[...], x))
    new = (x.astype(F32) + rows_of(u_ref) * sig).astype(BF)
    x_out[...] = new
    top = jax.nn.sigmoid(nn(gt_top_ref[...], new))
    y = turned(at_ref[1], mine_ref, other_ref)
    y_out[...] = y
    put_rows(pair_ref, nn(rt_ref[...], new), y.astype(F32) * top)


def gate_back(upper, x, u, gt, gu_ref, gg_ref):
    sig = jax.nn.sigmoid(nn(gt, x))
    put_rows(gu_ref, upper * sig)
    gg_ref[...] = (upper * u * sig * (1.0 - sig)).astype(BF)


def lower_of(y, gz, gg, r, g):
    return (y.astype(F32) + nn(r, gz) + nn(g, gg)).astype(BF)


def top_back_kernel(
    y_ref, pair_ref, x_top_ref, gt_top_ref, r_ref, g_ref, x_ref, u_ref, gt_ref, y_out, gg_top_out, gu_ref, gg_out
):
    y = y_ref[...]
    sig = jax.nn.sigmoid(nn(gt_top_ref[...], x_top_ref[...]))
    gg = (y.astype(F32) * rows_of(pair_ref, 0) * sig * (1.0 - sig)).astype(BF)
    gg_top_out[...] = gg
    lower = lower_of(y, rows_of(pair_ref, 1).astype(BF), gg, r_ref[...], g_ref[...])
    y_out[...] = lower
    gate_back(lower.astype(F32), x_ref[...], rows_of(u_ref), gt_ref[...], gu_ref, gg_out)


def back_kernel(y_ref, gz_ref, gg_ref, r_ref, g_ref, x_ref, u_ref, gt_ref, y_out, gu_ref, gg_out):
    gz = rows_of(gz_ref).astype(BF)
    lower = lower_of(y_ref[...], gz, gg_ref[...], r_ref[...], g_ref[...])
    y_out[...] = lower
    gate_back(lower.astype(F32), x_ref[...], rows_of(u_ref), gt_ref[...], gu_ref, gg_out)


def parts_of(x, gz, gg, z, gu, y):
    pt = feature_order(256, 256, True)
    qt = position_order(256, 256, True)
    x_n = nn(pt, x).astype(BF)
    gz_n = nn(pt, gz).astype(BF)
    gg_n = nn(pt, gg).astype(BF)
    z_n = nn(qt, z).astype(BF)
    gu_n = nn(qt, gu).astype(BF)
    y_n = nn(pt, y)
    lane = lax.broadcasted_iota(jnp.int32, (64, 128), 1)
    parts = []
    for i in range(2):
        at = slice(128 * i, 128 * i + 128)
        l_part = nt(z_n[at], gu_n[at])
        parts.append(
            (
                y_n[at].T,
                nt(x_n[at], gz_n[at]),
                nt(x_n[at], gg_n[at]),
                jnp.where(lane < 64, l_part[:64], l_part[64:]),
            )
        )
    return parts


def put_parts(parts, out_ref):
    for c in range(2):
        start = 0
        for part in parts[c]:
            stop = start + part.shape[0]
            out_ref[0, c, start:stop, :] = part.astype(BF)
            start = stop


def top_parts_kernel(x_ref, gave_ref, gg_ref, took_ref, y_ref, out_ref):
    gz = rows_of(gave_ref, 1).astype(BF)
    z = rows_of(took_ref, 0).astype(BF)
    gu = rows_of(took_ref, 1).astype(BF)
    put_parts(parts_of(x_ref[...], gz, gg_ref[...], z, gu, y_ref[...]), out_ref)


def parts_kernel(x_ref, gz_ref, gg_ref, z_ref, gu_ref, y_ref, held_ref, out_ref):
    gz = rows_of(gz_ref).astype(BF)
    z = rows_of(z_ref).astype(BF)
    gu = rows_of(gu_ref).astype(BF)
    put_parts(parts_of(x_ref[...], gz, gg_ref[...], z, gu, y_ref[...]), out_ref)


def last_kernel(x_ref, gz_ref, gg_ref, z_ref, gu_ref, y_ref, r_ref, g_ref, held_ref, out_ref):
    gz = rows_of(gz_ref).astype(BF)
    z = rows_of(z_ref).astype(BF)
    gu = rows_of(gu_ref).astype(BF)
    lower = lower_of(y_ref[...], gz, gg_ref[...], r_ref[...], g_ref[...])
    put_parts(parts_of(x_ref[...], gz, gg_ref[...], z, gu, lower), out_ref)


def settle_kernel(got_ref, y_out, r_out, g_out, l_out):
    n = y_out.shape[0] // 8
    total = None
    for i in range(8):
        y_out[n * i : n * i + n, :] = got_ref[i, :n, :]
        part = got_ref[i, n:, :].astype(F32)
        total = part if total is None else total + part
    r_out[...] = total[:128]
    g_out[...] = total[128:256]
    l_out[0] = total[256:, :64]
    l_out[1] = total[256:, 64:]


def run(kernel, outs, *args, dots=1, at=None, scratch=(), blocks=None):
    nbytes = sum(a.size * a.dtype.itemsize for a in args)
    params = pltpu.CompilerParams(vmem_limit_bytes=16 << 20)
    cost = pl.CostEstimate(
        flops=dots * 2 * 256 * 256 * 512, bytes_accessed=2 * nbytes, transcendentals=0
    )
    if at is None:
        return pl.pallas_call(
            kernel, out_shape=outs, compiler_params=params, cost_estimate=cost
        )(*args)
    specs = [
        spec or pl.BlockSpec(a.shape, lambda i, at, nd=a.ndim: (0,) * nd)
        for a, spec in zip(args, blocks or [None] * len(args))
    ]
    many = isinstance(outs, list)
    out_specs = [
        pl.BlockSpec(o.shape, lambda i, at, nd=len(o.shape): (0,) * nd)
        for o in (outs if many else [outs])
    ]
    return pl.pallas_call(
        kernel,
        out_shape=outs,
        grid_spec=pltpu.PrefetchScalarGridSpec(
            num_scalar_prefetch=1,
            grid=(1,),
            in_specs=specs,
            out_specs=out_specs if many else out_specs[0],
            scratch_shapes=list(scratch),
        ),
        compiler_params=params,
        cost_estimate=cost,
    )(at, *args)


def run_parts(kernel, layer, whole, *args):
    more = {} if layer == 3 else {"input_output_aliases": {len(args) - 1: 0}}
    specs = [pl.BlockSpec(a.shape, lambda i, nd=a.ndim: (0,) * nd) for a in args]
    if layer != 3:
        specs[-1] = pl.BlockSpec(memory_space=pl.ANY)
    return pl.pallas_call(
        kernel,
        out_shape=whole,
        grid=(1,),
        in_specs=specs,
        out_specs=pl.BlockSpec((1,) + whole.shape[1:], lambda i: (layer, 0, 0, 0)),
        compiler_params=pltpu.CompilerParams(vmem_limit_bytes=16 << 20),
        cost_estimate=pl.CostEstimate(
            flops=18 * 256 * 256 * 512, bytes_accessed=3 << 20, transcendentals=0
        ),
        **more,
    )(*args)


def sds(*shape, dtype=BF):
    return jax.ShapeDtypeStruct(shape, dtype)


def program(inputs, cotangent, r_weight, g_weight, l_weight):
    sections = lax.axis_size("x")
    tokens = inputs.shape[0] // (sections * 2)
    sect = lax.axis_index("x")
    core = lax.axis_index("c")
    at = jnp.stack([sect, core, sect * 2 + core]).astype(jnp.int32)

    def to_other(value):
        return lax.ppermute(value, "c", [(0, 1), (1, 0)])

    packed = pl.pallas_call(
        pack_kernel,
        out_shape=sds(320, 128),
        in_specs=[pl.BlockSpec(memory_space=pltpu.HBM)] * 3,
        out_specs=pl.BlockSpec(memory_space=pltpu.VMEM),
        scratch_shapes=[pltpu.VMEM((2, 64, 64), BF), pltpu.SemaphoreType.DMA((3,))],
        compiler_params=pltpu.CompilerParams(vmem_limit_bytes=67043328),
    )(r_weight, g_weight, l_weight)
    own = packed[None]
    for bit in (1, 3):
        arrived = lax.ppermute(own, "x", [(i, i ^ bit) for i in range(sections)])
        own = jnp.concatenate([own, arrived])
    other = to_other(own)

    def sent_over(whole):
        start = (sect * 2 + 1 - core) * tokens
        return to_other(lax.dynamic_slice_in_dim(whole, start, tokens, 0))

    def swap(block):
        return lax.all_to_all(block, ("y", "z"), 0, 0, tiled=True)

    flat = sds(256, tokens)
    sent = sds(32, 8, tokens)
    mine = pl.BlockSpec((tokens, 128), lambda i, at: (at[2], 0))
    outs = run(
        prepare_kernel,
        [sds(256, 256)] * 24,
        own,
        other,
        at=at,
        dots=24,
        scratch=[pltpu.VMEM((3, 256, 256), BF)],
    )
    mats = [outs[6 * s : 6 * s + 6] for s in range(sections)]
    from_other = sent_over(inputs)
    x0 = run(turn_kernel, flat, inputs, from_other, at=at, blocks=[mine, None])
    z = run(first_kernel, sent, x0, mats[0][1])
    crossed = sent_over(cotangent)
    z, crossed = lax.optimization_barrier((z, crossed))
    x = [x0]
    z_all, u_all = [], []
    last = sections - 1
    pair = sds(32, 16, tokens)
    for s in range(last):
        z = swap(z)
        z_all.append(z)
        u = swap(run(mix_kernel, sent, z, mats[s][5]))
        u_all.append(u)
        if s + 1 < last:
            new, z = run(gated_kernel, [flat, sent], x[s], u, mats[s][3], mats[s + 1][1], dots=2)
        else:
            new, both, y = run(
                top_kernel,
                [flat, pair, flat],
                x[s],
                u,
                mats[s][3],
                mats[last][1],
                cotangent,
                crossed,
                mats[last][3],
                dots=4,
                at=at,
                blocks=[None, None, None, None, mine, None, None],
            )
        x.append(new)
    took = swap(both)
    gave = swap(run(mix_both_kernel, pair, took, mats[last][5], mats[last][4], dots=2))
    y, gg_top, gu, gg = run(
        top_back_kernel,
        [flat, flat, sent, flat],
        y,
        gave,
        x[last],
        mats[last][3],
        mats[last][0],
        mats[last][2],
        x[last - 1],
        u_all[last - 1],
        mats[last - 1][3],
        dots=4,
    )
    whole = sds(sections, 2, tokens + 320, 128)
    parts = run_parts(top_parts_kernel, last, whole, x[last], gave, gg_top, took, y)
    for s in range(last - 1, -1, -1):
        gu, parts = lax.optimization_barrier((gu, parts))
        gu = swap(gu)
        gz = swap(run(mix_kernel, sent, gu, mats[s][4]))
        held = (x[s], gz, gg, z_all[s], gu)
        if s > 0:
            y, gu, gg = run(
                back_kernel,
                [flat, sent, flat],
                y,
                gz,
                gg,
                mats[s][0],
                mats[s][2],
                x[s - 1],
                u_all[s - 1],
                mats[s - 1][3],
                dots=3,
            )
            parts = run_parts(parts_kernel, s, whole, *held, y, parts)
    parts = run_parts(last_kernel, 0, whole, *held, y, mats[0][0], mats[0][2], parts)
    got = lax.all_to_all(
        parts.reshape(sections * 2, tokens + 320, 128), ("x", "c"), 0, 0, tiled=True
    )
    y_out, r_grad, g_grad, l_grad = run(
        settle_kernel,
        [
            sds(sections * 2 * tokens, 128),
            sds(128, 128, dtype=F32),
            sds(128, 128, dtype=F32),
            sds(2, 64, 64, dtype=F32),
        ],
        got,
    )
    return y_out[None], r_grad[None, None], g_grad[None, None], l_grad[None]


def solution(mesh):
    grid = Mesh(mesh.devices.reshape(4, 4, 8, 2), ("x", "y", "z", "c"))
    blk = ("y", "z", "c")
    return jax.shard_map(
        program,
        mesh=grid,
        in_specs=(
            P(None, blk),
            P(None, blk),
            P("x", blk, None, None),
            P("x", blk, None, None),
            P("x", blk, None, None),
        ),
        out_specs=(
            P("x", None, blk),
            P("x", blk, None, None),
            P("x", blk, None, None),
            P("x", blk, None, None),
        ),
        check_vma=False,
    )
```

```python
import jax
import jax.numpy as jnp
from jax import lax
from jax.experimental import pallas as pl
from jax.experimental.pallas import tpu as pltpu
from jax.sharding import Mesh, PartitionSpec as P

BF = jnp.bfloat16
F32 = jnp.float32


def nn(a, b):
    return lax.dot_general(a, b, (((1,), (0,)), ((), ())), preferred_element_type=F32)


def nt(a, b):
    return lax.dot_general(a, b, (((1,), (1,)), ((), ())), preferred_element_type=F32)


def feature_order(rows, cols, transposed=False, offset=0):
    r = lax.broadcasted_iota(jnp.int32, (rows, cols), 1 if transposed else 0)
    c = lax.broadcasted_iota(jnp.int32, (rows, cols), 0 if transposed else 1)
    natural = ((r >> 2) & 1) * 128 + (r >> 3) * 4 + (r & 3)
    return jnp.where(natural == c + offset, 1.0, 0.0).astype(BF)


def position_order(rows, cols, transposed=False):
    r = lax.broadcasted_iota(jnp.int32, (rows, cols), 1 if transposed else 0)
    c = lax.broadcasted_iota(jnp.int32, (rows, cols), 0 if transposed else 1)
    natural = (r & 3) * 64 + (r >> 3) * 2 + ((r >> 2) & 1)
    return jnp.where(natural == c, 1.0, 0.0).astype(BF)


def rows_of(ref, half=0):
    d, _, n = ref.shape
    return ref[:, 8 * half : 8 * half + 8, :].astype(F32).reshape(d * 8, n)


def put_rows(ref, *values):
    d, _, n = ref.shape
    slabs = [v.reshape(d, 8, n) for v in values]
    both = slabs[0] if len(slabs) == 1 else jnp.concatenate(slabs, axis=1)
    ref[...] = both.astype(ref.dtype)


def block_of(own_ref, other_ref, c, core, k, start, stop):
    mine = own_ref[k, start:stop, :].astype(F32)
    other = other_ref[k, start:stop, :].astype(F32)
    return jnp.where(core == c, mine, other)


def prepare_kernel(at_ref, *refs):
    shifted, other_ref = refs[:4], refs[4]
    outs, own_ref = refs[5:-1], refs[-1]
    sect, core = at_ref[0], at_ref[1]
    for k in range(4):
        own_ref[k] = shifted[k][...]
    p = feature_order(256, 256)
    q = position_order(256, 256)
    lane = lax.broadcasted_iota(jnp.int32, (64, 128), 1)
    for layer in range(4):
        k = lax.rem(sect - layer + 4, 4)
        r_out, rt_out, g_out, gt_out, l_out, lt_out = outs[6 * layer : 6 * layer + 6]
        for start, plain, flipped in ((0, r_out, rt_out), (128, g_out, gt_out)):
            blocks = [
                block_of(own_ref, other_ref, c, core, k, start, start + 128).astype(BF)
                for c in range(2)
            ]
            parts = [p[:, 128 * c : 128 * c + 128] for c in range(2)]
            left = jnp.concatenate([nn(parts[c], blocks[c]) for c in range(2)], axis=1).astype(BF)
            plain[...] = nt(left, p).astype(BF)
            left = jnp.concatenate([nt(parts[c], blocks[c]) for c in range(2)], axis=1).astype(BF)
            flipped[...] = nt(left, p).astype(BF)
        pairs = []
        for c in range(2):
            packed = block_of(own_ref, other_ref, c, core, k, 256, 320)
            low = jnp.where(lane < 64, packed, 0.0)
            high = jnp.where(lane < 64, 0.0, packed)
            pairs.append(jnp.concatenate([low, high], axis=0).astype(BF))
        parts = [q[:, 128 * c : 128 * c + 128] for c in range(2)]
        left = jnp.concatenate([nn(parts[c], pairs[c]) for c in range(2)], axis=1).astype(BF)
        l_out[...] = nt(left, q).astype(BF)
        left = jnp.concatenate([nt(parts[c], pairs[c]) for c in range(2)], axis=1).astype(BF)
        lt_out[...] = nt(left, q).astype(BF)


def turned(core, mine_ref, other_ref):
    p = feature_order(256, 128, offset=core * 128)
    o = feature_order(256, 128, offset=128 - core * 128)
    return (nt(p, mine_ref[...]) + nt(o, other_ref[...])).astype(BF)


def turn_kernel(at_ref, mine_ref, other_ref, x_ref):
    x_ref[...] = turned(at_ref[1], mine_ref, other_ref)


def first_kernel(x_ref, rt_ref, z_ref):
    put_rows(z_ref, nn(rt_ref[...], x_ref[...]))


def mix_kernel(z_ref, w_ref, u_ref):
    put_rows(u_ref, nn(w_ref[...], rows_of(z_ref).astype(BF)))


def gated_kernel(x_ref, u_ref, gt_ref, rt_ref, x_out, z_ref):
    x = x_ref[...]
    sig = jax.nn.sigmoid(nn(gt_ref[...], x))
    new = (x.astype(F32) + rows_of(u_ref) * sig).astype(BF)
    x_out[...] = new
    put_rows(z_ref, nn(rt_ref[...], new))


def mix_both_kernel(pair_ref, lt_ref, l_ref, out_ref):
    u = nn(lt_ref[...], rows_of(pair_ref, 0).astype(BF))
    gz = nn(l_ref[...], rows_of(pair_ref, 1).astype(BF))
    put_rows(out_ref, u, gz)


def top_kernel(
    at_ref, x_ref, u_ref, gt_ref, rt_ref, mine_ref, other_ref, gt_top_ref, x_out, pair_ref, y_out
):
    x = x_ref[...]
    sig = jax.nn.sigmoid(nn(gt_ref[...], x))
    new = (x.astype(F32) + rows_of(u_ref) * sig).astype(BF)
    x_out[...] = new
    top = jax.nn.sigmoid(nn(gt_top_ref[...], new))
    y = turned(at_ref[1], mine_ref, other_ref)
    y_out[...] = y
    put_rows(pair_ref, nn(rt_ref[...], new), y.astype(F32) * top)


def gate_back(upper, x, u, gt, gu_ref, gg_ref):
    sig = jax.nn.sigmoid(nn(gt, x))
    put_rows(gu_ref, upper * sig)
    gg_ref[...] = (upper * u * sig * (1.0 - sig)).astype(BF)


def lower_of(y, gz, gg, r, g):
    return (y.astype(F32) + nn(r, gz) + nn(g, gg)).astype(BF)


def top_back_kernel(
    y_ref, pair_ref, x_top_ref, gt_top_ref, r_ref, g_ref, x_ref, u_ref, gt_ref, y_out, gg_top_out, gu_ref, gg_out
):
    y = y_ref[...]
    sig = jax.nn.sigmoid(nn(gt_top_ref[...], x_top_ref[...]))
    gg = (y.astype(F32) * rows_of(pair_ref, 0) * sig * (1.0 - sig)).astype(BF)
    gg_top_out[...] = gg
    lower = lower_of(y, rows_of(pair_ref, 1).astype(BF), gg, r_ref[...], g_ref[...])
    y_out[...] = lower
    gate_back(lower.astype(F32), x_ref[...], rows_of(u_ref), gt_ref[...], gu_ref, gg_out)


def back_kernel(y_ref, gz_ref, gg_ref, r_ref, g_ref, x_ref, u_ref, gt_ref, y_out, gu_ref, gg_out):
    gz = rows_of(gz_ref).astype(BF)
    lower = lower_of(y_ref[...], gz, gg_ref[...], r_ref[...], g_ref[...])
    y_out[...] = lower
    gate_back(lower.astype(F32), x_ref[...], rows_of(u_ref), gt_ref[...], gu_ref, gg_out)


def parts_of(x, gz, gg, z, gu, y):
    pt = feature_order(256, 256, True)
    qt = position_order(256, 256, True)
    x_n = nn(pt, x).astype(BF)
    gz_n = nn(pt, gz).astype(BF)
    gg_n = nn(pt, gg).astype(BF)
    z_n = nn(qt, z).astype(BF)
    gu_n = nn(qt, gu).astype(BF)
    y_n = nn(pt, y)
    lane = lax.broadcasted_iota(jnp.int32, (64, 128), 1)
    parts = []
    for i in range(2):
        at = slice(128 * i, 128 * i + 128)
        l_part = nt(z_n[at], gu_n[at])
        parts.append(
            (
                y_n[at].T,
                nt(x_n[at], gz_n[at]),
                nt(x_n[at], gg_n[at]),
                jnp.where(lane < 64, l_part[:64], l_part[64:]),
            )
        )
    return parts


def put_parts(parts, out_ref):
    for c in range(2):
        start = 0
        for part in parts[c]:
            stop = start + part.shape[0]
            out_ref[0, c, start:stop, :] = part.astype(BF)
            start = stop


def top_parts_kernel(x_ref, gave_ref, gg_ref, took_ref, y_ref, out_ref):
    gz = rows_of(gave_ref, 1).astype(BF)
    z = rows_of(took_ref, 0).astype(BF)
    gu = rows_of(took_ref, 1).astype(BF)
    put_parts(parts_of(x_ref[...], gz, gg_ref[...], z, gu, y_ref[...]), out_ref)


def parts_kernel(x_ref, gz_ref, gg_ref, z_ref, gu_ref, y_ref, held_ref, out_ref):
    gz = rows_of(gz_ref).astype(BF)
    z = rows_of(z_ref).astype(BF)
    gu = rows_of(gu_ref).astype(BF)
    put_parts(parts_of(x_ref[...], gz, gg_ref[...], z, gu, y_ref[...]), out_ref)


def last_kernel(x_ref, gz_ref, gg_ref, z_ref, gu_ref, y_ref, r_ref, g_ref, held_ref, out_ref):
    gz = rows_of(gz_ref).astype(BF)
    z = rows_of(z_ref).astype(BF)
    gu = rows_of(gu_ref).astype(BF)
    lower = lower_of(y_ref[...], gz, gg_ref[...], r_ref[...], g_ref[...])
    put_parts(parts_of(x_ref[...], gz, gg_ref[...], z, gu, lower), out_ref)


def pick_kernel(at_ref, got_ref, out_ref):
    for i in range(4):
        out_ref[i] = got_ref[i, 1 - at_ref[1]]


def settle_kernel(at_ref, got_ref, other_ref, y_out, r_out, g_out, l_out):
    core = at_ref[1]
    n = y_out.shape[0] // 8
    total = None
    for i in range(4):
        here = pl.multiple_of((2 * i + core) * n, n)
        there = pl.multiple_of((2 * i + 1 - core) * n, n)
        y_out[pl.ds(here, n), :] = got_ref[i, core, :n, :]
        y_out[pl.ds(there, n), :] = other_ref[i, :n, :]
        part = got_ref[i, core, n:, :].astype(F32) + other_ref[i, n:, :].astype(F32)
        total = part if total is None else total + part
    r_out[...] = total[:128]
    g_out[...] = total[128:256]
    l_out[0] = total[256:, :64]
    l_out[1] = total[256:, 64:]


def run(kernel, outs, *args, dots=1, at=None, scratch=(), blocks=None):
    nbytes = sum(a.size * a.dtype.itemsize for a in args)
    params = pltpu.CompilerParams(vmem_limit_bytes=16 << 20)
    cost = pl.CostEstimate(
        flops=dots * 2 * 256 * 256 * 512, bytes_accessed=2 * nbytes, transcendentals=0
    )
    if at is None:
        return pl.pallas_call(
            kernel, out_shape=outs, compiler_params=params, cost_estimate=cost
        )(*args)
    specs = [
        spec or pl.BlockSpec(a.shape, lambda i, at, nd=a.ndim: (0,) * nd)
        for a, spec in zip(args, blocks or [None] * len(args))
    ]
    many = isinstance(outs, list)
    out_specs = [
        pl.BlockSpec(o.shape, lambda i, at, nd=len(o.shape): (0,) * nd)
        for o in (outs if many else [outs])
    ]
    return pl.pallas_call(
        kernel,
        out_shape=outs,
        grid_spec=pltpu.PrefetchScalarGridSpec(
            num_scalar_prefetch=1,
            grid=(1,),
            in_specs=specs,
            out_specs=out_specs if many else out_specs[0],
            scratch_shapes=list(scratch),
        ),
        compiler_params=params,
        cost_estimate=cost,
    )(at, *args)


def run_parts(kernel, layer, whole, *args):
    more = {} if layer == 3 else {"input_output_aliases": {len(args) - 1: 0}}
    specs = [pl.BlockSpec(a.shape, lambda i, nd=a.ndim: (0,) * nd) for a in args]
    if layer != 3:
        specs[-1] = pl.BlockSpec(memory_space=pl.ANY)
    return pl.pallas_call(
        kernel,
        out_shape=whole,
        grid=(1,),
        in_specs=specs,
        out_specs=pl.BlockSpec((1,) + whole.shape[1:], lambda i: (layer, 0, 0, 0)),
        compiler_params=pltpu.CompilerParams(vmem_limit_bytes=16 << 20),
        cost_estimate=pl.CostEstimate(
            flops=18 * 256 * 256 * 512, bytes_accessed=3 << 20, transcendentals=0
        ),
        **more,
    )(*args)


def sds(*shape, dtype=BF):
    return jax.ShapeDtypeStruct(shape, dtype)


def program(inputs, cotangent, r_weight, g_weight, l_weight):
    sections = lax.axis_size("x")
    tokens = inputs.shape[0] // (sections * 2)
    sect = lax.axis_index("x")
    core = lax.axis_index("c")
    at = jnp.stack([sect, core, sect * 2 + core]).astype(jnp.int32)

    def to_other(value):
        return lax.ppermute(value, "c", [(0, 1), (1, 0)])

    def shift(value, k):
        return lax.ppermute(value, "x", [(i, (i + k) % sections) for i in range(sections)])

    l_flat = jnp.concatenate([l_weight[0, 0], l_weight[0, 1]], axis=1)
    packed = jnp.concatenate([r_weight[0, 0], g_weight[0, 0], l_flat], axis=0)
    own = [packed]
    for k in range(1, sections):
        own.append(shift(packed, k))
    other = to_other(jnp.stack(own))

    def sent_over(whole):
        start = (sect * 2 + 1 - core) * tokens
        return to_other(lax.dynamic_slice_in_dim(whole, start, tokens, 0))

    def swap(block):
        return lax.all_to_all(block, ("y", "z"), 0, 0, tiled=True)

    flat = sds(256, tokens)
    sent = sds(32, 8, tokens)
    mine = pl.BlockSpec((tokens, 128), lambda i, at: (at[2], 0))
    outs = run(
        prepare_kernel,
        [sds(256, 256)] * 24,
        *own,
        other,
        at=at,
        dots=24,
        scratch=[pltpu.VMEM((4, 320, 128), BF)],
    )
    mats = [outs[6 * s : 6 * s + 6] for s in range(sections)]
    from_other = sent_over(inputs)
    x0 = run(turn_kernel, flat, inputs, from_other, at=at, blocks=[mine, None])
    z = run(first_kernel, sent, x0, mats[0][1])
    crossed = sent_over(cotangent)
    z, crossed = lax.optimization_barrier((z, crossed))
    x = [x0]
    z_all, u_all = [], []
    last = sections - 1
    pair = sds(32, 16, tokens)
    for s in range(last):
        z = swap(z)
        z_all.append(z)
        u = swap(run(mix_kernel, sent, z, mats[s][5]))
        u_all.append(u)
        if s + 1 < last:
            new, z = run(gated_kernel, [flat, sent], x[s], u, mats[s][3], mats[s + 1][1], dots=2)
        else:
            new, both, y = run(
                top_kernel,
                [flat, pair, flat],
                x[s],
                u,
                mats[s][3],
                mats[last][1],
                cotangent,
                crossed,
                mats[last][3],
                dots=4,
                at=at,
                blocks=[None, None, None, None, mine, None, None],
            )
        x.append(new)
    took = swap(both)
    gave = swap(run(mix_both_kernel, pair, took, mats[last][5], mats[last][4], dots=2))
    y, gg_top, gu, gg = run(
        top_back_kernel,
        [flat, flat, sent, flat],
        y,
        gave,
        x[last],
        mats[last][3],
        mats[last][0],
        mats[last][2],
        x[last - 1],
        u_all[last - 1],
        mats[last - 1][3],
        dots=4,
    )
    whole = sds(sections, 2, tokens + 320, 128)
    parts = run_parts(top_parts_kernel, last, whole, x[last], gave, gg_top, took, y)
    for s in range(last - 1, -1, -1):
        gu, parts = lax.optimization_barrier((gu, parts))
        gu = swap(gu)
        gz = swap(run(mix_kernel, sent, gu, mats[s][4]))
        held = (x[s], gz, gg, z_all[s], gu)
        if s > 0:
            y, gu, gg = run(
                back_kernel,
                [flat, sent, flat],
                y,
                gz,
                gg,
                mats[s][0],
                mats[s][2],
                x[s - 1],
                u_all[s - 1],
                mats[s - 1][3],
                dots=3,
            )
            parts = run_parts(parts_kernel, s, whole, *held, y, parts)
    parts = run_parts(last_kernel, 0, whole, *held, y, mats[0][0], mats[0][2], parts)
    got = lax.all_to_all(parts, "x", 0, 0, tiled=True)
    other = to_other(run(pick_kernel, sds(sections, tokens + 320, 128), got, at=at))
    y_out, r_grad, g_grad, l_grad = run(
        settle_kernel,
        [
            sds(sections * 2 * tokens, 128),
            sds(128, 128, dtype=F32),
            sds(128, 128, dtype=F32),
            sds(2, 64, 64, dtype=F32),
        ],
        got,
        other,
        at=at,
    )
    return y_out[None], r_grad[None, None], g_grad[None, None], l_grad[None]


def solution(mesh):
    grid = Mesh(mesh.devices.reshape(4, 4, 8, 2), ("x", "y", "z", "c"))
    blk = ("y", "z", "c")
    return jax.shard_map(
        program,
        mesh=grid,
        in_specs=(
            P(None, blk),
            P(None, blk),
            P("x", blk, None, None),
            P("x", blk, None, None),
            P("x", blk, None, None),
        ),
        out_specs=(
            P("x", None, blk),
            P("x", blk, None, None),
            P("x", blk, None, None),
            P("x", blk, None, None),
        ),
        check_vma=False,
    )
```

```python
import functools

import jax
import jax.numpy as jnp
from jax import lax
from jax.experimental import pallas as pl
from jax.experimental.pallas import tpu as pltpu
from jax.sharding import Mesh, PartitionSpec as P

BF = jnp.bfloat16
F32 = jnp.float32


def nn(a, b):
    return lax.dot_general(a, b, (((1,), (0,)), ((), ())), preferred_element_type=F32)


def nt(a, b):
    return lax.dot_general(a, b, (((1,), (1,)), ((), ())), preferred_element_type=F32)


def feature_order(rows, cols, transposed=False, offset=0):
    r = lax.broadcasted_iota(jnp.int32, (rows, cols), 1 if transposed else 0)
    c = lax.broadcasted_iota(jnp.int32, (rows, cols), 0 if transposed else 1)
    natural = ((r >> 2) & 1) * 128 + (r >> 3) * 4 + (r & 3)
    return jnp.where(natural == c + offset, 1.0, 0.0).astype(BF)


def position_order(rows, cols, transposed=False):
    r = lax.broadcasted_iota(jnp.int32, (rows, cols), 1 if transposed else 0)
    c = lax.broadcasted_iota(jnp.int32, (rows, cols), 0 if transposed else 1)
    natural = (r & 3) * 64 + (r >> 3) * 2 + ((r >> 2) & 1)
    return jnp.where(natural == c, 1.0, 0.0).astype(BF)


def rows_of(ref, half=0):
    d, _, n = ref.shape
    return ref[:, 8 * half : 8 * half + 8, :].astype(F32).reshape(d * 8, n)


def put_rows(ref, *values):
    d, _, n = ref.shape
    slabs = [v.reshape(d, 8, n) for v in values]
    both = slabs[0] if len(slabs) == 1 else jnp.concatenate(slabs, axis=1)
    ref[...] = both.astype(ref.dtype)


def block_of(own_ref, other_ref, c, core, k, start, stop):
    mine = own_ref[k, start:stop, :].astype(F32)
    other = other_ref[k, start:stop, :].astype(F32)
    return jnp.where(core == c, mine, other)


def prepare_kernel(at_ref, *refs):
    shifted, other_ref = refs[:4], refs[4]
    outs, own_ref = refs[5:-1], refs[-1]
    sect, core = at_ref[0], at_ref[1]
    for k in range(4):
        own_ref[k] = shifted[k][...]
    p = feature_order(256, 256)
    q = position_order(256, 256)
    lane = lax.broadcasted_iota(jnp.int32, (64, 128), 1)
    for layer in range(4):
        k = lax.rem(sect - layer + 4, 4)
        r_out, rt_out, g_out, gt_out, l_out, lt_out = outs[6 * layer : 6 * layer + 6]
        for start, plain, flipped in ((0, r_out, rt_out), (128, g_out, gt_out)):
            blocks = [
                block_of(own_ref, other_ref, c, core, k, start, start + 128).astype(BF)
                for c in range(2)
            ]
            parts = [p[:, 128 * c : 128 * c + 128] for c in range(2)]
            left = jnp.concatenate([nn(parts[c], blocks[c]) for c in range(2)], axis=1).astype(BF)
            plain[...] = nt(left, p).astype(BF)
            left = jnp.concatenate([nt(parts[c], blocks[c]) for c in range(2)], axis=1).astype(BF)
            flipped[...] = nt(left, p).astype(BF)
        pairs = []
        for c in range(2):
            packed = block_of(own_ref, other_ref, c, core, k, 256, 320)
            low = jnp.where(lane < 64, packed, 0.0)
            high = jnp.where(lane < 64, 0.0, packed)
            pairs.append(jnp.concatenate([low, high], axis=0).astype(BF))
        parts = [q[:, 128 * c : 128 * c + 128] for c in range(2)]
        left = jnp.concatenate([nn(parts[c], pairs[c]) for c in range(2)], axis=1).astype(BF)
        l_out[...] = nt(left, q).astype(BF)
        left = jnp.concatenate([nt(parts[c], pairs[c]) for c in range(2)], axis=1).astype(BF)
        lt_out[...] = nt(left, q).astype(BF)


def turned(at_ref, whole_ref, other_ref):
    core = at_ref[1]
    n = other_ref.shape[0]
    mine = whole_ref[pl.ds(pl.multiple_of(at_ref[2] * n, n), n), :]
    other = other_ref[...]
    p = feature_order(256, 128, offset=core * 128)
    o = feature_order(256, 128, offset=128 - core * 128)
    return (nt(p, mine) + nt(o, other)).astype(BF)


def turn_kernel(at_ref, mine_ref, other_ref, x_ref):
    x_ref[...] = turned(at_ref, mine_ref, other_ref)


def first_kernel(x_ref, rt_ref, z_ref):
    put_rows(z_ref, nn(rt_ref[...], x_ref[...]))


def mix_kernel(z_ref, w_ref, u_ref):
    put_rows(u_ref, nn(w_ref[...], rows_of(z_ref).astype(BF)))


def gated_kernel(x_ref, u_ref, gt_ref, rt_ref, x_out, z_ref):
    x = x_ref[...]
    sig = jax.nn.sigmoid(nn(gt_ref[...], x))
    new = (x.astype(F32) + rows_of(u_ref) * sig).astype(BF)
    x_out[...] = new
    put_rows(z_ref, nn(rt_ref[...], new))


def mix_both_kernel(pair_ref, lt_ref, l_ref, out_ref):
    u = nn(lt_ref[...], rows_of(pair_ref, 0).astype(BF))
    gz = nn(l_ref[...], rows_of(pair_ref, 1).astype(BF))
    put_rows(out_ref, u, gz)


def top_kernel(
    at_ref, x_ref, u_ref, gt_ref, rt_ref, mine_ref, other_ref, gt_top_ref, x_out, pair_ref, y_out
):
    x = x_ref[...]
    sig = jax.nn.sigmoid(nn(gt_ref[...], x))
    new = (x.astype(F32) + rows_of(u_ref) * sig).astype(BF)
    x_out[...] = new
    top = jax.nn.sigmoid(nn(gt_top_ref[...], new))
    y = turned(at_ref, mine_ref, other_ref)
    y_out[...] = y
    put_rows(pair_ref, nn(rt_ref[...], new), y.astype(F32) * top)


def gate_back(upper, x, u, gt, gu_ref, gg_ref):
    sig = jax.nn.sigmoid(nn(gt, x))
    put_rows(gu_ref, upper * sig)
    gg_ref[...] = (upper * u * sig * (1.0 - sig)).astype(BF)


def lower_of(y, gz, gg, r, g):
    return (y.astype(F32) + nn(r, gz) + nn(g, gg)).astype(BF)


def top_back_kernel(
    y_ref, pair_ref, x_top_ref, gt_top_ref, r_ref, g_ref, x_ref, u_ref, gt_ref, y_out, gg_top_out, gu_ref, gg_out
):
    y = y_ref[...]
    sig = jax.nn.sigmoid(nn(gt_top_ref[...], x_top_ref[...]))
    gg = (y.astype(F32) * rows_of(pair_ref, 0) * sig * (1.0 - sig)).astype(BF)
    gg_top_out[...] = gg
    lower = lower_of(y, rows_of(pair_ref, 1).astype(BF), gg, r_ref[...], g_ref[...])
    y_out[...] = lower
    gate_back(lower.astype(F32), x_ref[...], rows_of(u_ref), gt_ref[...], gu_ref, gg_out)


def back_kernel(y_ref, gz_ref, gg_ref, r_ref, g_ref, x_ref, u_ref, gt_ref, y_out, gu_ref, gg_out):
    gz = rows_of(gz_ref).astype(BF)
    lower = lower_of(y_ref[...], gz, gg_ref[...], r_ref[...], g_ref[...])
    y_out[...] = lower
    gate_back(lower.astype(F32), x_ref[...], rows_of(u_ref), gt_ref[...], gu_ref, gg_out)


def parts_of(x, gz, gg, z, gu, y):
    pt = feature_order(256, 256, True)
    qt = position_order(256, 256, True)
    x_n = nn(pt, x).astype(BF)
    gz_n = nn(pt, gz).astype(BF)
    gg_n = nn(pt, gg).astype(BF)
    z_n = nn(qt, z).astype(BF)
    gu_n = nn(qt, gu).astype(BF)
    y_n = nn(pt, y)
    lane = lax.broadcasted_iota(jnp.int32, (64, 128), 1)
    parts = []
    for i in range(2):
        at = slice(128 * i, 128 * i + 128)
        l_part = nt(z_n[at], gu_n[at])
        parts.append(
            (
                y_n[at].T,
                nt(x_n[at], gz_n[at]),
                nt(x_n[at], gg_n[at]),
                jnp.where(lane < 64, l_part[:64], l_part[64:]),
            )
        )
    return parts


def put_parts(parts, layer, out_ref):
    for c in range(2):
        start = 0
        for part in parts[c]:
            stop = start + part.shape[0]
            out_ref[layer, c, start:stop, :] = part.astype(BF)
            start = stop


def top_parts_kernel(layer, x_ref, gave_ref, gg_ref, took_ref, y_ref, out_ref):
    gz = rows_of(gave_ref, 1).astype(BF)
    z = rows_of(took_ref, 0).astype(BF)
    gu = rows_of(took_ref, 1).astype(BF)
    put_parts(parts_of(x_ref[...], gz, gg_ref[...], z, gu, y_ref[...]), layer, out_ref)


def parts_kernel(layer, x_ref, gz_ref, gg_ref, z_ref, gu_ref, y_ref, held_ref, out_ref):
    gz = rows_of(gz_ref).astype(BF)
    z = rows_of(z_ref).astype(BF)
    gu = rows_of(gu_ref).astype(BF)
    put_parts(parts_of(x_ref[...], gz, gg_ref[...], z, gu, y_ref[...]), layer, out_ref)


def last_kernel(layer, x_ref, gz_ref, gg_ref, z_ref, gu_ref, y_ref, r_ref, g_ref, held_ref, out_ref):
    gz = rows_of(gz_ref).astype(BF)
    z = rows_of(z_ref).astype(BF)
    gu = rows_of(gu_ref).astype(BF)
    lower = lower_of(y_ref[...], gz, gg_ref[...], r_ref[...], g_ref[...])
    put_parts(parts_of(x_ref[...], gz, gg_ref[...], z, gu, lower), layer, out_ref)


def pick_kernel(at_ref, got_ref, out_ref):
    for i in range(4):
        out_ref[i] = got_ref[i, 1 - at_ref[1]]


def settle_kernel(at_ref, got_ref, other_ref, y_out, r_out, g_out, l_out):
    core = at_ref[1]
    n = y_out.shape[0] // 8
    total = None
    for i in range(4):
        here = pl.multiple_of((2 * i + core) * n, n)
        there = pl.multiple_of((2 * i + 1 - core) * n, n)
        y_out[pl.ds(here, n), :] = got_ref[i, core, :n, :]
        y_out[pl.ds(there, n), :] = other_ref[i, :n, :]
        part = got_ref[i, core, n:, :].astype(F32) + other_ref[i, n:, :].astype(F32)
        total = part if total is None else total + part
    r_out[...] = total[:128]
    g_out[...] = total[128:256]
    l_out[0] = total[256:, :64]
    l_out[1] = total[256:, 64:]


def run(kernel, outs, *args, dots=1, at=None, scratch=(), aliases=None):
    nbytes = sum(a.size * a.dtype.itemsize for a in args)
    specs = [pl.BlockSpec(memory_space=pltpu.VMEM)] * len(args)
    if at is not None:
        args = (at,) + args
        specs = [pl.BlockSpec(memory_space=pltpu.SMEM)] + specs
    return pl.pallas_call(
        kernel,
        out_shape=outs,
        in_specs=specs,
        scratch_shapes=list(scratch),
        input_output_aliases=aliases or {},
        compiler_params=pltpu.CompilerParams(vmem_limit_bytes=16 << 20),
        cost_estimate=pl.CostEstimate(
            flops=dots * 2 * 256 * 256 * 512, bytes_accessed=2 * nbytes, transcendentals=0
        ),
    )(*args)


def run_parts(kernel, layer, whole, *args):
    aliases = {} if layer == 3 else {len(args) - 1: 0}
    return run(functools.partial(kernel, layer), whole, *args, dots=9, aliases=aliases)


def sds(*shape, dtype=BF):
    return jax.ShapeDtypeStruct(shape, dtype)


def program(inputs, cotangent, r_weight, g_weight, l_weight):
    sections = lax.axis_size("x")
    tokens = inputs.shape[0] // (sections * 2)
    sect = lax.axis_index("x")
    core = lax.axis_index("c")
    at = jnp.stack([sect, core, sect * 2 + core]).astype(jnp.int32)

    def to_other(value):
        return lax.ppermute(value, "c", [(0, 1), (1, 0)])

    def shift(value, k):
        return lax.ppermute(value, "x", [(i, (i + k) % sections) for i in range(sections)])

    l_flat = jnp.concatenate([l_weight[0, 0], l_weight[0, 1]], axis=1)
    packed = jnp.concatenate([r_weight[0, 0], g_weight[0, 0], l_flat], axis=0)
    own = [packed]
    for k in range(1, sections):
        own.append(shift(packed, k))
    other = to_other(jnp.stack(own))

    def sent_over(whole):
        start = (sect * 2 + 1 - core) * tokens
        return to_other(lax.dynamic_slice_in_dim(whole, start, tokens, 0))

    def swap(block):
        return lax.all_to_all(block, ("y", "z"), 0, 0, tiled=True)

    flat = sds(256, tokens)
    sent = sds(32, 8, tokens)
    outs = run(
        prepare_kernel,
        [sds(256, 256)] * 24,
        *own,
        other,
        at=at,
        dots=24,
        scratch=[pltpu.VMEM((4, 320, 128), BF)],
    )
    mats = [outs[6 * s : 6 * s + 6] for s in range(sections)]
    from_other = sent_over(inputs)
    x0 = run(turn_kernel, flat, inputs, from_other, at=at)
    z = run(first_kernel, sent, x0, mats[0][1])
    crossed = sent_over(cotangent)
    z, crossed = lax.optimization_barrier((z, crossed))
    x = [x0]
    z_all, u_all = [], []
    last = sections - 1
    pair = sds(32, 16, tokens)
    for s in range(last):
        z = swap(z)
        z_all.append(z)
        u = swap(run(mix_kernel, sent, z, mats[s][5]))
        u_all.append(u)
        if s + 1 < last:
            new, z = run(gated_kernel, [flat, sent], x[s], u, mats[s][3], mats[s + 1][1], dots=2)
        else:
            new, both, y = run(
                top_kernel,
                [flat, pair, flat],
                x[s],
                u,
                mats[s][3],
                mats[last][1],
                cotangent,
                crossed,
                mats[last][3],
                dots=4,
                at=at,
            )
        x.append(new)
    took = swap(both)
    gave = swap(run(mix_both_kernel, pair, took, mats[last][5], mats[last][4], dots=2))
    y, gg_top, gu, gg = run(
        top_back_kernel,
        [flat, flat, sent, flat],
        y,
        gave,
        x[last],
        mats[last][3],
        mats[last][0],
        mats[last][2],
        x[last - 1],
        u_all[last - 1],
        mats[last - 1][3],
        dots=4,
    )
    whole = sds(sections, 2, tokens + 320, 128)
    parts = run_parts(top_parts_kernel, last, whole, x[last], gave, gg_top, took, y)
    for s in range(last - 1, -1, -1):
        gu, parts = lax.optimization_barrier((gu, parts))
        gu = swap(gu)
        gz = swap(run(mix_kernel, sent, gu, mats[s][4]))
        held = (x[s], gz, gg, z_all[s], gu)
        if s > 0:
            y, gu, gg = run(
                back_kernel,
                [flat, sent, flat],
                y,
                gz,
                gg,
                mats[s][0],
                mats[s][2],
                x[s - 1],
                u_all[s - 1],
                mats[s - 1][3],
                dots=3,
            )
            parts = run_parts(parts_kernel, s, whole, *held, y, parts)
    parts = run_parts(last_kernel, 0, whole, *held, y, mats[0][0], mats[0][2], parts)
    got = lax.all_to_all(parts, "x", 0, 0, tiled=True)
    other = to_other(run(pick_kernel, sds(sections, tokens + 320, 128), got, at=at))
    y_out, r_grad, g_grad, l_grad = run(
        settle_kernel,
        [
            sds(sections * 2 * tokens, 128),
            sds(128, 128, dtype=F32),
            sds(128, 128, dtype=F32),
            sds(2, 64, 64, dtype=F32),
        ],
        got,
        other,
        at=at,
    )
    return y_out[None], r_grad[None, None], g_grad[None, None], l_grad[None]


def solution(mesh):
    grid = Mesh(mesh.devices.reshape(4, 4, 8, 2), ("x", "y", "z", "c"))
    blk = ("y", "z", "c")
    return jax.shard_map(
        program,
        mesh=grid,
        in_specs=(
            P(None, blk),
            P(None, blk),
            P("x", blk, None, None),
            P("x", blk, None, None),
            P("x", blk, None, None),
        ),
        out_specs=(
            P("x", None, blk),
            P("x", blk, None, None),
            P("x", blk, None, None),
            P("x", blk, None, None),
        ),
        check_vma=False,
    )
```

```python
import functools

import jax
import jax.numpy as jnp
from jax import lax
from jax.experimental import pallas as pl
from jax.experimental.pallas import tpu as pltpu
from jax.sharding import Mesh, PartitionSpec as P

BF = jnp.bfloat16
F32 = jnp.float32


def nn(a, b):
    return lax.dot_general(a, b, (((1,), (0,)), ((), ())), preferred_element_type=F32)


def nt(a, b):
    return lax.dot_general(a, b, (((1,), (1,)), ((), ())), preferred_element_type=F32)


def place_of(slot):
    return (slot & 3) * 8 + (slot >> 2)


def feature_order(rows, cols, transposed=False, offset=0):
    r = lax.broadcasted_iota(jnp.int32, (rows, cols), 1 if transposed else 0)
    c = lax.broadcasted_iota(jnp.int32, (rows, cols), 0 if transposed else 1)
    natural = ((r >> 2) & 1) * 128 + place_of(r >> 3) * 4 + (r & 3)
    return jnp.where(natural == c + offset, 1.0, 0.0).astype(BF)


def position_order(rows, cols, transposed=False):
    r = lax.broadcasted_iota(jnp.int32, (rows, cols), 1 if transposed else 0)
    c = lax.broadcasted_iota(jnp.int32, (rows, cols), 0 if transposed else 1)
    natural = (r & 3) * 64 + place_of(r >> 3) * 2 + ((r >> 2) & 1)
    return jnp.where(natural == c, 1.0, 0.0).astype(BF)


def rows_of(ref, half=0):
    d, _, n = ref.shape
    return ref[:, 8 * half : 8 * half + 8, :].astype(F32).reshape(d * 8, n)


def put_rows(ref, *values):
    d, _, n = ref.shape
    slabs = [v.reshape(d, 8, n) for v in values]
    both = slabs[0] if len(slabs) == 1 else jnp.concatenate(slabs, axis=1)
    ref[...] = both.astype(ref.dtype)


def block_of(own_ref, other_ref, c, core, k, start, stop):
    mine = own_ref[k, start:stop, :].astype(F32)
    other = other_ref[k, start:stop, :].astype(F32)
    return jnp.where(core == c, mine, other)


def prepare_kernel(at_ref, *refs):
    shifted, other_ref = refs[:4], refs[4]
    outs, own_ref = refs[5:-1], refs[-1]
    sect, core = at_ref[0], at_ref[1]
    for k in range(4):
        own_ref[k] = shifted[k][...]
    p = feature_order(256, 256)
    q = position_order(256, 256)
    lane = lax.broadcasted_iota(jnp.int32, (64, 128), 1)
    for layer in range(4):
        k = lax.rem(sect - layer + 4, 4)
        r_out, rt_out, g_out, gt_out, l_out, lt_out = outs[6 * layer : 6 * layer + 6]
        for start, plain, flipped in ((0, r_out, rt_out), (128, g_out, gt_out)):
            blocks = [
                block_of(own_ref, other_ref, c, core, k, start, start + 128).astype(BF)
                for c in range(2)
            ]
            parts = [p[:, 128 * c : 128 * c + 128] for c in range(2)]
            left = jnp.concatenate([nn(parts[c], blocks[c]) for c in range(2)], axis=1).astype(BF)
            plain[...] = nt(left, p).astype(BF)
            left = jnp.concatenate([nt(parts[c], blocks[c]) for c in range(2)], axis=1).astype(BF)
            flipped[...] = nt(left, p).astype(BF)
        pairs = []
        for c in range(2):
            packed = block_of(own_ref, other_ref, c, core, k, 256, 320)
            low = jnp.where(lane < 64, packed, 0.0)
            high = jnp.where(lane < 64, 0.0, packed)
            pairs.append(jnp.concatenate([low, high], axis=0).astype(BF))
        parts = [q[:, 128 * c : 128 * c + 128] for c in range(2)]
        left = jnp.concatenate([nn(parts[c], pairs[c]) for c in range(2)], axis=1).astype(BF)
        l_out[...] = nt(left, q).astype(BF)
        left = jnp.concatenate([nt(parts[c], pairs[c]) for c in range(2)], axis=1).astype(BF)
        lt_out[...] = nt(left, q).astype(BF)


def turned(at_ref, whole_ref, other_ref):
    core = at_ref[1]
    n = other_ref.shape[0]
    mine = whole_ref[pl.ds(pl.multiple_of(at_ref[2] * n, n), n), :]
    other = other_ref[...]
    p = feature_order(256, 128, offset=core * 128)
    o = feature_order(256, 128, offset=128 - core * 128)
    return (nt(p, mine) + nt(o, other)).astype(BF)


def turn_kernel(at_ref, mine_ref, other_ref, x_ref):
    x_ref[...] = turned(at_ref, mine_ref, other_ref)


def first_kernel(x_ref, rt_ref, z_ref):
    put_rows(z_ref, nn(rt_ref[...], x_ref[...]))


def mix_kernel(z_ref, w_ref, u_ref):
    put_rows(u_ref, nn(w_ref[...], rows_of(z_ref).astype(BF)))


def gated_kernel(x_ref, u_ref, gt_ref, rt_ref, x_out, z_ref):
    x = x_ref[...]
    sig = jax.nn.sigmoid(nn(gt_ref[...], x))
    new = (x.astype(F32) + rows_of(u_ref) * sig).astype(BF)
    x_out[...] = new
    put_rows(z_ref, nn(rt_ref[...], new))


def mix_both_kernel(pair_ref, lt_ref, l_ref, out_ref):
    u = nn(lt_ref[...], rows_of(pair_ref, 0).astype(BF))
    gz = nn(l_ref[...], rows_of(pair_ref, 1).astype(BF))
    put_rows(out_ref, u, gz)


def top_kernel(
    at_ref, x_ref, u_ref, gt_ref, rt_ref, mine_ref, other_ref, gt_top_ref, x_out, pair_ref, y_out
):
    x = x_ref[...]
    sig = jax.nn.sigmoid(nn(gt_ref[...], x))
    new = (x.astype(F32) + rows_of(u_ref) * sig).astype(BF)
    x_out[...] = new
    top = jax.nn.sigmoid(nn(gt_top_ref[...], new))
    y = turned(at_ref, mine_ref, other_ref)
    y_out[...] = y
    put_rows(pair_ref, nn(rt_ref[...], new), y.astype(F32) * top)


def gate_back(upper, x, u, gt, gu_ref, gg_ref):
    sig = jax.nn.sigmoid(nn(gt, x))
    put_rows(gu_ref, upper * sig)
    gg_ref[...] = (upper * u * sig * (1.0 - sig)).astype(BF)


def lower_of(y, gz, gg, r, g):
    return (y.astype(F32) + nn(r, gz) + nn(g, gg)).astype(BF)


def top_back_kernel(
    y_ref, pair_ref, x_top_ref, gt_top_ref, r_ref, g_ref, x_ref, u_ref, gt_ref, y_out, gg_top_out, gu_ref, gg_out
):
    y = y_ref[...]
    sig = jax.nn.sigmoid(nn(gt_top_ref[...], x_top_ref[...]))
    gg = (y.astype(F32) * rows_of(pair_ref, 0) * sig * (1.0 - sig)).astype(BF)
    gg_top_out[...] = gg
    lower = lower_of(y, rows_of(pair_ref, 1).astype(BF), gg, r_ref[...], g_ref[...])
    y_out[...] = lower
    gate_back(lower.astype(F32), x_ref[...], rows_of(u_ref), gt_ref[...], gu_ref, gg_out)


def back_kernel(y_ref, gz_ref, gg_ref, r_ref, g_ref, x_ref, u_ref, gt_ref, y_out, gu_ref, gg_out):
    gz = rows_of(gz_ref).astype(BF)
    lower = lower_of(y_ref[...], gz, gg_ref[...], r_ref[...], g_ref[...])
    y_out[...] = lower
    gate_back(lower.astype(F32), x_ref[...], rows_of(u_ref), gt_ref[...], gu_ref, gg_out)


def parts_of(x, gz, gg, z, gu, y):
    pt = feature_order(256, 256, True)
    qt = position_order(256, 256, True)
    x_n = nn(pt, x).astype(BF)
    gz_n = nn(pt, gz).astype(BF)
    gg_n = nn(pt, gg).astype(BF)
    z_n = nn(qt, z).astype(BF)
    gu_n = nn(qt, gu).astype(BF)
    y_n = nn(pt, y)
    lane = lax.broadcasted_iota(jnp.int32, (64, 128), 1)
    parts = []
    for i in range(2):
        at = slice(128 * i, 128 * i + 128)
        l_part = nt(z_n[at], gu_n[at])
        parts.append(
            (
                y_n[at].T,
                nt(x_n[at], gz_n[at]),
                nt(x_n[at], gg_n[at]),
                jnp.where(lane < 64, l_part[:64], l_part[64:]),
            )
        )
    return parts


def put_parts(parts, layer, out_ref):
    for c in range(2):
        start = 0
        for part in parts[c]:
            stop = start + part.shape[0]
            out_ref[layer, c, start:stop, :] = part.astype(BF)
            start = stop


def top_parts_kernel(layer, x_ref, gave_ref, gg_ref, took_ref, y_ref, out_ref):
    gz = rows_of(gave_ref, 1).astype(BF)
    z = rows_of(took_ref, 0).astype(BF)
    gu = rows_of(took_ref, 1).astype(BF)
    put_parts(parts_of(x_ref[...], gz, gg_ref[...], z, gu, y_ref[...]), layer, out_ref)


def parts_kernel(layer, x_ref, gz_ref, gg_ref, z_ref, gu_ref, y_ref, held_ref, out_ref):
    gz = rows_of(gz_ref).astype(BF)
    z = rows_of(z_ref).astype(BF)
    gu = rows_of(gu_ref).astype(BF)
    put_parts(parts_of(x_ref[...], gz, gg_ref[...], z, gu, y_ref[...]), layer, out_ref)


def last_kernel(layer, x_ref, gz_ref, gg_ref, z_ref, gu_ref, y_ref, r_ref, g_ref, held_ref, out_ref):
    gz = rows_of(gz_ref).astype(BF)
    z = rows_of(z_ref).astype(BF)
    gu = rows_of(gu_ref).astype(BF)
    lower = lower_of(y_ref[...], gz, gg_ref[...], r_ref[...], g_ref[...])
    put_parts(parts_of(x_ref[...], gz, gg_ref[...], z, gu, lower), layer, out_ref)


def pick_kernel(at_ref, got_ref, out_ref):
    for i in range(4):
        out_ref[i] = got_ref[i, 1 - at_ref[1]]


def settle_kernel(at_ref, got_ref, other_ref, y_out, r_out, g_out, l_out):
    core = at_ref[1]
    n = y_out.shape[0] // 8
    total = None
    for i in range(4):
        here = pl.multiple_of((2 * i + core) * n, n)
        there = pl.multiple_of((2 * i + 1 - core) * n, n)
        y_out[pl.ds(here, n), :] = got_ref[i, core, :n, :]
        y_out[pl.ds(there, n), :] = other_ref[i, :n, :]
        part = got_ref[i, core, n:, :].astype(F32) + other_ref[i, n:, :].astype(F32)
        total = part if total is None else total + part
    r_out[...] = total[:128]
    g_out[...] = total[128:256]
    l_out[0] = total[256:, :64]
    l_out[1] = total[256:, 64:]


def run(kernel, outs, *args, dots=1, at=None, scratch=(), aliases=None):
    nbytes = sum(a.size * a.dtype.itemsize for a in args)
    specs = [pl.BlockSpec(memory_space=pltpu.VMEM)] * len(args)
    if at is not None:
        args = (at,) + args
        specs = [pl.BlockSpec(memory_space=pltpu.SMEM)] + specs
    return pl.pallas_call(
        kernel,
        out_shape=outs,
        in_specs=specs,
        scratch_shapes=list(scratch),
        input_output_aliases=aliases or {},
        compiler_params=pltpu.CompilerParams(vmem_limit_bytes=16 << 20),
        cost_estimate=pl.CostEstimate(
            flops=dots * 2 * 256 * 256 * 512, bytes_accessed=2 * nbytes, transcendentals=0
        ),
    )(*args)


def run_parts(kernel, layer, whole, *args):
    aliases = {} if layer == 3 else {len(args) - 1: 0}
    return run(functools.partial(kernel, layer), whole, *args, dots=9, aliases=aliases)


def sds(*shape, dtype=BF):
    return jax.ShapeDtypeStruct(shape, dtype)


def program(inputs, cotangent, r_weight, g_weight, l_weight):
    sections = lax.axis_size("x")
    tokens = inputs.shape[0] // (sections * 2)
    sect = lax.axis_index("x")
    core = lax.axis_index("c")
    at = jnp.stack([sect, core, sect * 2 + core]).astype(jnp.int32)

    def to_other(value):
        return lax.ppermute(value, "c", [(0, 1), (1, 0)])

    def shift(value, k):
        return lax.ppermute(value, "x", [(i, (i + k) % sections) for i in range(sections)])

    l_flat = jnp.concatenate([l_weight[0, 0], l_weight[0, 1]], axis=1)
    packed = jnp.concatenate([r_weight[0, 0], g_weight[0, 0], l_flat], axis=0)
    own = [packed]
    for k in range(1, sections):
        own.append(shift(packed, k))
    other = to_other(jnp.stack(own))

    def sent_over(whole):
        start = (sect * 2 + 1 - core) * tokens
        return to_other(lax.dynamic_slice_in_dim(whole, start, tokens, 0))

    def swap(block):
        return lax.all_to_all(block, ("z", "y"), 0, 0, tiled=True)

    flat = sds(256, tokens)
    sent = sds(32, 8, tokens)
    outs = run(
        prepare_kernel,
        [sds(256, 256)] * 24,
        *own,
        other,
        at=at,
        dots=24,
        scratch=[pltpu.VMEM((4, 320, 128), BF)],
    )
    mats = [outs[6 * s : 6 * s + 6] for s in range(sections)]
    from_other = sent_over(inputs)
    x0 = run(turn_kernel, flat, inputs, from_other, at=at)
    z = run(first_kernel, sent, x0, mats[0][1])
    crossed = sent_over(cotangent)
    z, crossed = lax.optimization_barrier((z, crossed))
    x = [x0]
    z_all, u_all = [], []
    last = sections - 1
    pair = sds(32, 16, tokens)
    for s in range(last):
        z = swap(z)
        z_all.append(z)
        u = swap(run(mix_kernel, sent, z, mats[s][5]))
        u_all.append(u)
        if s + 1 < last:
            new, z = run(gated_kernel, [flat, sent], x[s], u, mats[s][3], mats[s + 1][1], dots=2)
        else:
            new, both, y = run(
                top_kernel,
                [flat, pair, flat],
                x[s],
                u,
                mats[s][3],
                mats[last][1],
                cotangent,
                crossed,
                mats[last][3],
                dots=4,
                at=at,
            )
        x.append(new)
    took = swap(both)
    gave = swap(run(mix_both_kernel, pair, took, mats[last][5], mats[last][4], dots=2))
    y, gg_top, gu, gg = run(
        top_back_kernel,
        [flat, flat, sent, flat],
        y,
        gave,
        x[last],
        mats[last][3],
        mats[last][0],
        mats[last][2],
        x[last - 1],
        u_all[last - 1],
        mats[last - 1][3],
        dots=4,
    )
    whole = sds(sections, 2, tokens + 320, 128)
    parts = run_parts(top_parts_kernel, last, whole, x[last], gave, gg_top, took, y)
    for s in range(last - 1, -1, -1):
        gu, parts = lax.optimization_barrier((gu, parts))
        gu = swap(gu)
        gz = swap(run(mix_kernel, sent, gu, mats[s][4]))
        held = (x[s], gz, gg, z_all[s], gu)
        if s > 0:
            y, gu, gg = run(
                back_kernel,
                [flat, sent, flat],
                y,
                gz,
                gg,
                mats[s][0],
                mats[s][2],
                x[s - 1],
                u_all[s - 1],
                mats[s - 1][3],
                dots=3,
            )
            parts = run_parts(parts_kernel, s, whole, *held, y, parts)
    parts = run_parts(last_kernel, 0, whole, *held, y, mats[0][0], mats[0][2], parts)
    got = lax.all_to_all(parts, "x", 0, 0, tiled=True)
    other = to_other(run(pick_kernel, sds(sections, tokens + 320, 128), got, at=at))
    y_out, r_grad, g_grad, l_grad = run(
        settle_kernel,
        [
            sds(sections * 2 * tokens, 128),
            sds(128, 128, dtype=F32),
            sds(128, 128, dtype=F32),
            sds(2, 64, 64, dtype=F32),
        ],
        got,
        other,
        at=at,
    )
    return y_out[None], r_grad[None, None], g_grad[None, None], l_grad[None]


def solution(mesh):
    grid = Mesh(mesh.devices.reshape(4, 4, 8, 2), ("x", "y", "z", "c"))
    blk = ("y", "z", "c")
    return jax.shard_map(
        program,
        mesh=grid,
        in_specs=(
            P(None, blk),
            P(None, blk),
            P("x", blk, None, None),
            P("x", blk, None, None),
            P("x", blk, None, None),
        ),
        out_specs=(
            P("x", None, blk),
            P("x", blk, None, None),
            P("x", blk, None, None),
            P("x", blk, None, None),
        ),
        check_vma=False,
    )
```
